128 devices in a mesh: seq: 32 (over z, y, x_hi), ch: 4 (over x_lo, core).
Axes of the slice: x: 4 (x_hi: 2, x_lo: 2; x = x_hi * 2 + x_lo), y: 4, z: 4, core: 2. Of those that a mesh axis runs over, the one named last changes fastest.
Arguments:
- attn_query: bfloat16 [4096, 4096], P(('seq', 'ch')), may hold values from -6 to 6
- attn_key: bfloat16 [4096, 4096], P(('seq', 'ch')), may hold values from -6 to 6
- attn_value: bfloat16 [4096, 4096], P(('seq', 'ch')), may hold values from -6 to 6
- attn_output: bfloat16 [4096, 4096], P(('seq', 'ch')), may hold values from -1.796875 to 1.796875
- attn_grad_out: bfloat16 [4096, 4096], P(('seq', 'ch')), may hold values from -6 to 6
- conv_query: bfloat16 [4096, 8192], P(('seq', 'ch')), may hold values from -6 to 6
- conv_key: bfloat16 [4096, 8192], P(('seq', 'ch')), may hold values from -6 to 6
- conv_value: bfloat16 [4096, 8192], P(('seq', 'ch')), may hold values from -6 to 6
- conv_grad_out: bfloat16 [4096, 8192], P(('seq', 'ch')), may hold values from -6 to 6
- conv_filter: bfloat16 [512, 128], P('ch'), may hold values from -0.5 to 0.5
- doc_lengths: int32 [12], replicated, may hold values from 1 to 1280, 4096 in all
Outputs:
- grad_attn_query: bfloat16 [4096, 4096], P(('seq', 'ch'))
- grad_attn_key: bfloat16 [4096, 4096], P(('seq', 'ch'))
- grad_attn_value: bfloat16 [4096, 4096], P(('seq', 'ch'))
- grad_conv_query: bfloat16 [4096, 8192], P(('seq', 'ch'))
- grad_conv_key: bfloat16 [4096, 8192], P(('seq', 'ch'))
- grad_conv_value: bfloat16 [4096, 8192], P(('seq', 'ch'))
- grad_filter: float32 [512, 128], P('ch')
The draws below stay inside these ranges and needn't reach their ends.
Inputs may be any that keep to these rules, and one draw needn't show every extreme that they name: `doc_lengths`: the lengths of 12 documents laid end to end in the window; they sum to 4096 and the longest has exactly 1280 positions.
All inputs are finite; a program needn't handle non-finite values.
Results may differ from the reference program's by a relative error of at most 0.0049.
Values may be sent and summed in bfloat16 or wider, within the bound.
A program may use at most 128 MiB of HBM per device.

```python
import math
import jax
import jax.numpy as jnp
import numpy as np
from jax import lax

HEADS = 32
HEAD_DIM = 128
CHANNELS = 8192
GROUP = 16
FILTER_LEN = 128
DOCS = 12
TOKENS = 4096
MOST = 1280


def draw_attn_query(key, part):
    base_key = jax.random.fold_in(key, 1)
    values = jnp.clip(jax.random.normal(base_key, (TOKENS, HEADS, HEAD_DIM), jnp.float32), -4.0, 4.0)
    return values.reshape(TOKENS, HEADS * HEAD_DIM).astype(jnp.bfloat16)


def draw_attn_key(key, part):
    base_key = jax.random.fold_in(key, 2)
    values = jnp.clip(jax.random.normal(base_key, (TOKENS, HEADS, HEAD_DIM), jnp.float32), -4.0, 4.0)
    return values.reshape(TOKENS, HEADS * HEAD_DIM).astype(jnp.bfloat16)


def block_levels(key, dims, shards, smallest, top_value):
    def one(dim, parts):
        draws = jax.random.uniform(jax.random.fold_in(jax.random.fold_in(key, 6), dim), (parts,), jnp.float32, smallest / len(shards), top_value / len(shards))
        return jnp.repeat(jnp.exp(draws), dims[dim] // parts).reshape((-1,) + (1,) * (len(dims) - dim - 1))

    gain = one(*shards[0])
    for cut in shards[1:]:
        gain = gain * one(*cut)
    return gain


def length_profile(number_of, total, reach, skew):
    loads = [(1 << 20) // math.isqrt(standing ** skew) + 1 for standing in range(2, number_of + 1)]
    rest, counts = total - reach - (number_of - 1), [1] * (number_of - 1)
    while rest > 0:
        free = [i for i in range(number_of - 1) if counts[i] < reach]
        pool, remaining = sum([loads[i] for i in free]), rest
        for i in free:
            more = min(reach - counts[i], max(1, remaining * loads[i] // pool), rest)
            counts[i] = counts[i] + more
            rest = rest - more
    return np.array([reach] + counts)


def uneven(rng, number_of, total, most, slope):
    if number_of == 2:
        one = jax.random.randint(rng, (), max(1, total - most), min(most, total - 1) + 1)
        return jnp.stack([one, total - one])
    tallies = jnp.asarray(length_profile(number_of, total, most, slope), jnp.int32)
    couples = (number_of - 1) // 2
    giver, receiver = tallies[1:1 + 2 * couples:2], tallies[2:2 + 2 * couples:2]
    slack = jnp.minimum(giver - 1, most - receiver)
    passed = jax.random.randint(jax.random.fold_in(rng, 1), (couples,), 0, 1 << 20) % (slack + 1)
    tallies = tallies.at[1:1 + 2 * couples:2].set(giver - passed).at[2:2 + 2 * couples:2].set(receiver + passed)
    return tallies[jax.random.permutation(jax.random.fold_in(rng, 2), number_of)]


def centred(own_key, shape, deviation, bound, cuts=(), held_as=jnp.bfloat16):
    factor_of = block_levels(own_key, shape, cuts, -0.22, 0.18) if cuts else 1.0
    drawn = jax.random.normal(own_key, shape, jnp.float32) * deviation * factor_of
    return jnp.minimum(jnp.maximum(drawn, -bound), bound).astype(held_as)


def setup_inputs(seed: int = 0) -> dict:
    keys = jax.random.split(jax.random.key(seed), 12)
    attn_query = draw_attn_query(jax.random.fold_in(keys[11], 71), 0)
    attn_key = draw_attn_key(jax.random.fold_in(keys[11], 71), 0)
    attn_value = centred(keys[2], (TOKENS, HEADS * HEAD_DIM), 1.0, 6.0, ((0, 128),))
    attn_output = centred(keys[3], (TOKENS, HEADS * HEAD_DIM), 0.3, 1.796875, ((0, 128),))
    attn_grad_out = centred(keys[4], (TOKENS, HEADS * HEAD_DIM), 1.0, 6.0, ((0, 128),))
    conv_query = centred(keys[5], (TOKENS, CHANNELS), 1.0, 6.0, ((0, 128),))
    conv_key = centred(keys[6], (TOKENS, CHANNELS), 1.0, 6.0, ((0, 128),))
    conv_value = centred(keys[7], (TOKENS, CHANNELS), 1.0, 6.0, ((0, 128),))
    conv_grad_out = centred(keys[8], (TOKENS, CHANNELS), 1.0, 6.0, ((0, 128),))
    conv_filter = centred(keys[9], (CHANNELS // GROUP, FILTER_LEN), FILTER_LEN ** -0.5, 0.5, ((0, 4),))
    doc_lengths = uneven(keys[10], DOCS, TOKENS, MOST, 2).astype(jnp.int32)
    return dict(attn_query=attn_query, attn_key=attn_key, attn_value=attn_value, attn_output=attn_output, attn_grad_out=attn_grad_out, conv_query=conv_query, conv_key=conv_key, conv_value=conv_value, conv_grad_out=conv_grad_out, conv_filter=conv_filter, doc_lengths=doc_lengths)


def doc_index(doc_lengths, positions):
    doc_ends = jnp.cumsum(doc_lengths).astype(jnp.int32)
    return jnp.sum((doc_ends[None, :] <= positions[:, None]).astype(jnp.int32), axis=1)


def reference(attn_query, attn_key, attn_value, attn_output, attn_grad_out, conv_query, conv_key, conv_value, conv_grad_out, conv_filter, doc_lengths):
    scale_factor = 1.0 / (HEAD_DIM ** 0.5)
    positions = jnp.arange(TOKENS, dtype=jnp.int32)
    doc_ids = doc_index(doc_lengths, positions)
    visible = (doc_ids[:, None] == doc_ids[None, :]) & (positions[None, :] <= positions[:, None])

    def per_head(head_slices):
        head_query, head_key, head_value, head_output, head_grad = head_slices
        scores = jnp.dot(head_query, head_key.T, preferred_element_type=jnp.float32) * scale_factor
        row_max = jnp.max(jnp.where(visible, scores, -jnp.inf), axis=1)
        totals = jnp.sum(jnp.where(visible, jnp.exp(scores - row_max[:, None]), 0.0), axis=1)
        log_norm = row_max + jnp.log(totals)
        probs = jnp.where(visible, jnp.exp(scores - log_norm[:, None]), 0.0)
        delta = jnp.sum(head_grad.astype(jnp.float32) * head_output.astype(jnp.float32), axis=1)
        grad_probs = jnp.dot(head_grad, head_value.T, preferred_element_type=jnp.float32)
        grad_scores = probs * (grad_probs - delta[:, None])
        grad_query = jnp.dot(grad_scores, head_key.astype(jnp.float32), precision=lax.Precision.HIGHEST) * scale_factor
        grad_key = jnp.dot(grad_scores.T, head_query.astype(jnp.float32), precision=lax.Precision.HIGHEST) * scale_factor
        grad_value = jnp.dot(probs.T, head_grad.astype(jnp.float32), precision=lax.Precision.HIGHEST)
        return (grad_query, grad_key, grad_value)

    def to_heads(array):
        return array.reshape(TOKENS, HEADS, HEAD_DIM).transpose(1, 0, 2)

    def from_heads(array):
        return array.transpose(1, 0, 2).reshape(TOKENS, HEADS * HEAD_DIM).astype(jnp.bfloat16)

    grad_q_heads, grad_k_heads, grad_v_heads = lax.map(per_head, (to_heads(attn_query), to_heads(attn_key), to_heads(attn_value), to_heads(attn_output), to_heads(attn_grad_out)))

    mixed_rounded = (conv_key.astype(jnp.float32) * conv_value.astype(jnp.float32)).astype(jnp.bfloat16)
    mixed = lax.optimization_barrier(mixed_rounded).astype(jnp.float32)
    out_grad_rounded = (conv_grad_out.astype(jnp.float32) * conv_query.astype(jnp.float32)).astype(jnp.bfloat16)
    out_grad = lax.optimization_barrier(out_grad_rounded).astype(jnp.float32)
    channel_taps = jnp.repeat(conv_filter.astype(jnp.float32), GROUP, axis=0)
    before = jnp.concatenate((jnp.zeros((FILTER_LEN, CHANNELS), jnp.float32), mixed), axis=0)
    after = jnp.concatenate((out_grad, jnp.zeros((FILTER_LEN, CHANNELS), jnp.float32)), axis=0)
    doc_before = jnp.concatenate((jnp.full((FILTER_LEN,), -1, jnp.int32), doc_ids), axis=0)
    doc_after = jnp.concatenate((doc_ids, jnp.full((FILTER_LEN,), -1, jnp.int32)), axis=0)

    def tap_step(tap_index, carried):
        conv_out, mixed_grad, tap_grads = carried
        tap_at = jnp.asarray(tap_index).astype(jnp.int32)
        back_start = (jnp.int32(FILTER_LEN) - tap_at).astype(jnp.int32)
        earlier = lax.dynamic_slice_in_dim(before, back_start, TOKENS, 0)
        earlier_doc = lax.dynamic_slice_in_dim(doc_before, back_start, TOKENS, 0)
        back_valid = (earlier_doc == doc_ids)[:, None]
        tap_row = lax.dynamic_slice_in_dim(channel_taps, tap_at, 1, 1)[:, 0]
        conv_out = conv_out + jnp.where(back_valid, earlier * tap_row[None, :], 0.0)
        tap_sum = jnp.sum(jnp.where(back_valid, out_grad * earlier, 0.0), axis=0)
        tap_grads = lax.dynamic_update_slice_in_dim(tap_grads, tap_sum[None, :], tap_at, 0)
        later = lax.dynamic_slice_in_dim(after, tap_at, TOKENS, 0)
        later_doc = lax.dynamic_slice_in_dim(doc_after, tap_at, TOKENS, 0)
        ahead_valid = (later_doc == doc_ids)[:, None]
        mixed_grad = mixed_grad + jnp.where(ahead_valid, later * tap_row[None, :], 0.0)
        return (conv_out, mixed_grad, tap_grads)

    start_state = (jnp.zeros((TOKENS, CHANNELS), jnp.float32), jnp.zeros((TOKENS, CHANNELS), jnp.float32), jnp.zeros((FILTER_LEN, CHANNELS), jnp.float32))
    conv_out, mixed_grad, tap_grads = lax.fori_loop(0, FILTER_LEN, tap_step, start_state)
    grad_conv_query = (conv_grad_out.astype(jnp.float32) * conv_out).astype(jnp.bfloat16)
    grad_conv_key = (mixed_grad * conv_value.astype(jnp.float32)).astype(jnp.bfloat16)
    grad_conv_value = (mixed_grad * conv_key.astype(jnp.float32)).astype(jnp.bfloat16)
    grad_filter = jnp.sum(tap_grads.reshape(FILTER_LEN, CHANNELS // GROUP, GROUP), axis=2).T
    return (from_heads(grad_q_heads), from_heads(grad_k_heads), from_heads(grad_v_heads), grad_conv_query, grad_conv_key, grad_conv_value, grad_filter)
```

```python
import functools
import math

import jax
import jax.numpy as jnp
from jax import lax
from jax.experimental import pallas as pl
from jax.experimental.pallas import tpu as pltpu
from jax.sharding import PartitionSpec as P

MESH = pl.DeviceIdType.MESH
HEAD_DIM = 128
FILTER_LEN = 128
DOCS = 12
PLANE = 32
PLANES = 4
ROWS = 32
SPAN = PLANE * ROWS
TILE = 256
NEAR = SPAN // TILE
REACH = 5
WINDOW = SPAN + REACH * TILE
CONV_WIDTH = 256
CONV_GROUPS = 16
LOG2_SCALE = math.log2(math.e) / math.sqrt(HEAD_DIM)
SCALE = 1.0 / math.sqrt(HEAD_DIM)
NEG_FILL = -1e30
VMEM_LIMIT = 60 * 1024 * 1024


def place_in_slice():
    me = lax.axis_index("seq") * 4 + lax.axis_index("ch")
    return lax.div(me, PLANE), lax.rem(me, PLANE)


def device_of(z, p):
    return (z * (PLANE // 4) + lax.div(p, 4), lax.rem(p, 4))


def conv_block(p):
    return lax.rem(p, 4) * (PLANE // 4) + lax.div(p, 4)


def greet(z, p):
    barrier = pltpu.get_barrier_semaphore()

    def hello(k, carried):
        pl.semaphore_signal(
            barrier, inc=1, device_id=device_of(z, lax.rem(p + k, PLANE)), device_id_type=MESH
        )
        return carried

    lax.fori_loop(1, PLANE, hello, 0)
    for step in range(1, PLANES):
        pl.semaphore_signal(
            barrier, inc=1, device_id=device_of(lax.rem(z + step, PLANES), p), device_id_type=MESH
        )
    pl.semaphore_wait(barrier, PLANE - 1 + PLANES - 1)


def wait_bytes(ref, sem):
    pltpu.make_async_copy(ref, ref, sem).wait()


def spread_kernel(
    q, k, v, o, g, mix, og, qw, kw, vw, ow, gw, mw, ogw, send_sem, recv_sem, zsend_sem, zrecv_sem
):
    z, p = place_in_slice()
    greet(z, p)

    def send(slot, src, dst, base, width, block):
        mine = dst.at[pl.ds(pl.multiple_of(base + p * ROWS, ROWS), ROWS), :]

        def columns(r):
            return src.at[:, pl.ds(pl.multiple_of(block(r) * width, width), width)]

        pltpu.make_async_copy(columns(p), mine, recv_sem.at[slot]).start()

        def step(i, carried):
            r = lax.rem(p + i, PLANE)
            pltpu.make_async_remote_copy(
                src_ref=columns(r),
                dst_ref=mine,
                send_sem=send_sem.at[slot],
                recv_sem=recv_sem.at[slot],
                device_id=device_of(z, r),
                device_id_type=MESH,
            ).start()
            return carried

        lax.fori_loop(1, PLANE, step, 0)

    hops = []

    def hop(slot, ref, src_row, dst_row, count, step):
        copy = pltpu.make_async_remote_copy(
            src_ref=ref.at[pl.ds(src_row, count), :],
            dst_ref=ref.at[pl.ds(dst_row, count), :],
            send_sem=zsend_sem.at[slot],
            recv_sem=zrecv_sem.at[slot],
            device_id=device_of(lax.rem(z + step, PLANES), p),
            device_id_type=MESH,
        )
        copy.start()
        hops.append(copy)

    def arrived(slot, dst, base):
        wait_bytes(dst.at[pl.ds(base, SPAN), :], recv_sem.at[slot])

    head = lambda r: r
    back = REACH * TILE
    send(0, k, kw, back, HEAD_DIM, head)
    send(1, v, vw, back, HEAD_DIM, head)
    send(2, q, qw, 0, HEAD_DIM, head)
    send(3, g, gw, 0, HEAD_DIM, head)
    for slot, ref in ((0, kw), (1, vw)):
        arrived(slot, ref, back)
        hop(2 * slot, ref, back, TILE, SPAN, 1)
        hop(2 * slot + 1, ref, SPAN + back - TILE, 0, TILE, 2)
    send(5, mix, mw, FILTER_LEN, CONV_WIDTH, conv_block)
    for slot, ref in ((2, qw), (3, gw)):
        arrived(slot, ref, 0)
        hop(2 * slot, ref, 0, SPAN, SPAN, 3)
        hop(2 * slot + 1, ref, 0, 2 * SPAN, TILE, 2)
    send(6, og, ogw, 0, CONV_WIDTH, conv_block)
    send(4, o, ow, 0, HEAD_DIM, head)
    arrived(5, mw, FILTER_LEN)
    hop(8, mw, SPAN, 0, FILTER_LEN, 1)
    arrived(6, ogw, 0)
    hop(9, ogw, 0, SPAN, FILTER_LEN, 3)
    arrived(4, ow, 0)
    rest = SPAN - ROWS
    for slot, ref in enumerate((kw, vw, qw, gw, ow, mw, ogw)):
        wait_bytes(ref.at[pl.ds(0, rest), :], send_sem.at[slot])
    for copy in hops:
        copy.wait()


def spread(q, k, v, o, g, mix, og):
    bf16 = jnp.bfloat16
    any_space = pl.BlockSpec(memory_space=pl.ANY)
    window = jax.ShapeDtypeStruct((WINDOW, HEAD_DIM), bf16)
    conv = jax.ShapeDtypeStruct((SPAN + FILTER_LEN, CONV_WIDTH), bf16)
    return pl.pallas_call(
        spread_kernel,
        out_shape=(
            window,
            window,
            window,
            jax.ShapeDtypeStruct((SPAN, HEAD_DIM), bf16),
            window,
            conv,
            conv,
        ),
        in_specs=[any_space] * 7,
        out_specs=(any_space,) * 7,
        scratch_shapes=[
            pltpu.SemaphoreType.DMA((7,)),
            pltpu.SemaphoreType.DMA((7,)),
            pltpu.SemaphoreType.DMA((10,)),
            pltpu.SemaphoreType.DMA((10,)),
        ],
        compiler_params=pltpu.CompilerParams(collective_id=0, has_side_effects=True),
        name="spread",
    )(q, k, v, o, g, mix, og)


def doc_ends(len_ref):
    ends = []
    total = jnp.int32(0)
    for d in range(DOCS):
        total = total + len_ref[d]
        ends.append(total)
    return ends


def doc_start(ends, pos):
    start = jnp.zeros_like(pos)
    for end in ends:
        start = jnp.maximum(start, jnp.where(end <= pos, end, 0))
    return start


def doc_stop(ends, pos):
    stop = jnp.full_like(pos, ends[-1])
    for end in ends:
        stop = jnp.minimum(stop, jnp.where(end > pos, end, ends[-1]))
    return stop


def nt_dot(a, b):
    return lax.dot_general(a, b, (((1,), (1,)), ((), ())), preferred_element_type=jnp.float32)


def tile_rows(ref, i):
    return ref[pl.ds(pl.multiple_of(i * TILE, TILE), TILE), :]


def row_positions(base):
    return base + lax.broadcasted_iota(jnp.int32, (1, TILE), 1)


def first_tile(ends, z, q_base):
    start = doc_start(ends, q_base)
    return lax.div(start - (z * SPAN - REACH * TILE), TILE)


def seen_before(z, kb, starts):
    k_pos = z * SPAN - REACH * TILE + kb * TILE + lax.broadcasted_iota(jnp.int32, (TILE, TILE), 0)
    return k_pos >= starts


def seen_diagonal(z, kb, starts):
    below = lax.broadcasted_iota(jnp.int32, (TILE, TILE), 0) <= lax.broadcasted_iota(
        jnp.int32, (TILE, TILE), 1
    )
    return seen_before(z, kb, starts) & below


def stats_kernel(len_ref, qw, kw, gw, ow, out_ref):
    z, _ = place_in_slice()
    ends = doc_ends(len_ref)

    def query_tile(qi, carried):
        q_base = z * SPAN + qi * TILE
        starts = doc_start(ends, row_positions(q_base))
        query = tile_rows(qw, qi)

        def scores(kb, seen):
            s = nt_dot(tile_rows(kw, kb), query) * LOG2_SCALE
            return jnp.where(seen(z, kb, starts), s, NEG_FILL)

        s = scores(qi + REACH, seen_diagonal)
        top = jnp.max(s, axis=0, keepdims=True)
        total = jnp.sum(jnp.exp2(s - top), axis=0, keepdims=True)

        def key_tile(kb, state):
            top, total = state
            s = scores(kb, seen_before)
            new_top = jnp.maximum(top, jnp.max(s, axis=0, keepdims=True))
            total = total * jnp.exp2(top - new_top) + jnp.sum(
                jnp.exp2(s - new_top), axis=0, keepdims=True
            )
            return new_top, total

        top, total = lax.fori_loop(
            first_tile(ends, z, q_base), qi + REACH, key_tile, (top, total)
        )
        product = tile_rows(gw, qi).astype(jnp.float32) * tile_rows(ow, qi).astype(jnp.float32)
        out_ref[qi, 0:1, :] = top + jnp.log2(total)
        out_ref[qi, 1:2, :] = jnp.sum(product.T, axis=0, keepdims=True)
        return carried

    lax.fori_loop(0, NEAR, query_tile, 0)


def grads_kernel(
    len_ref, qw, kw, vw, gw, own_stats, near_stats, far_stats, dq, dk, dv, stats, dk_sum, dv_sum, dq_sum
):
    z, _ = place_in_slice()
    ends = doc_ends(len_ref)
    stats[0:NEAR] = own_stats[...]
    stats[NEAR : 2 * NEAR] = near_stats[...]
    stats[2 * NEAR : 2 * NEAR + 1] = far_stats[...]
    dk_sum[...] = jnp.zeros_like(dk_sum)
    dv_sum[...] = jnp.zeros_like(dv_sum)

    def pair(qi, kb, starts, seen, for_query, for_key):
        query = tile_rows(qw, qi)
        grad = tile_rows(gw, qi)
        key = tile_rows(kw, kb)
        s = nt_dot(key, query) * LOG2_SCALE - stats[qi, 0:1, :]
        probs = jnp.where(seen(z, kb, starts), jnp.exp2(s), 0.0)
        grad_scores = probs * (nt_dot(tile_rows(vw, kb), grad) - stats[qi, 1:2, :])
        grad_scores = grad_scores.astype(jnp.bfloat16)
        if for_key:
            rows = pl.ds(pl.multiple_of((kb - REACH) * TILE, TILE), TILE)
            dv_sum[rows, :] += jnp.dot(
                probs.astype(jnp.bfloat16), grad, preferred_element_type=jnp.float32
            )
            dk_sum[rows, :] += jnp.dot(grad_scores, query, preferred_element_type=jnp.float32)
        if for_query:
            dq_sum[...] += lax.dot_general(
                key, grad_scores, (((0,), (0,)), ((), ())), preferred_element_type=jnp.float32
            )

    def own_tile(qi, carried):
        q_base = z * SPAN + qi * TILE
        starts = doc_start(ends, row_positions(q_base))
        first = first_tile(ends, z, q_base)
        dq_sum[...] = jnp.zeros_like(dq_sum)

        def before(kb, inner):
            pair(qi, kb, starts, seen_before, True, False)
            return inner

        def within(kb, inner):
            pair(qi, kb, starts, seen_before, True, True)
            return inner

        lax.fori_loop(first, REACH, before, 0)
        lax.fori_loop(jnp.maximum(first, REACH), REACH + qi, within, 0)
        pair(qi, REACH + qi, starts, seen_diagonal, True, True)
        rows = pl.ds(pl.multiple_of(qi * TILE, TILE), TILE)
        dq[rows, :] = (dq_sum[...].T * SCALE).astype(jnp.bfloat16)
        return carried

    lax.fori_loop(0, NEAR, own_tile, 0)

    def later_tile(qi, carried):
        q_base = z * SPAN + qi * TILE
        starts = doc_start(ends, row_positions(q_base))

        def after(kb, inner):
            pair(qi, kb, starts, seen_before, False, True)
            return inner

        first = jnp.maximum(first_tile(ends, z, q_base), REACH)
        lax.fori_loop(first, REACH + NEAR, after, 0)
        return carried

    lax.fori_loop(NEAR, NEAR + REACH, later_tile, 0)
    dk[...] = (dk_sum[...] * SCALE).astype(jnp.bfloat16)
    dv[...] = dv_sum[...].astype(jnp.bfloat16)


def conv_kernel(len_ref, taps, back_taps, mw, ogw, out_ref, grad_ref, tap_ref, circ, back_circ, tap_sum):
    z, _ = place_in_slice()
    ends = doc_ends(len_ref)
    size = FILTER_LEN
    bf16 = jnp.bfloat16
    for group in range(CONV_GROUPS):
        for src, dst in ((taps, circ), (back_taps, back_circ)):
            row = jnp.broadcast_to(src[group : group + 1, :], (size, size))
            dst[group] = pltpu.roll(row, 0, 1, stride=1, stride_axis=0).astype(bf16)
    tap_sum[...] = jnp.zeros_like(tap_sum)
    down = lax.broadcasted_iota(jnp.int32, (size, size), 0)
    across = lax.broadcasted_iota(jnp.int32, (size, size), 1)
    group_of_lane = lax.div(across, 16)

    def block(tb, carried):
        base = z * SPAN + tb * size
        positions = base + lax.broadcasted_iota(jnp.int32, (1, size), 1)

        def as_column(row):
            return jnp.broadcast_to(row.astype(jnp.float32), (size, size)).T.astype(jnp.int32)

        start = as_column(doc_start(ends, positions))
        stop = as_column(doc_stop(ends, positions))
        prev = jnp.where((across > down) & (base - size + across >= start), 1.0, 0.0)
        here = jnp.where((across <= down) & (base + across >= start), 1.0, 0.0)
        ahead = jnp.where((across >= down) & (base + across < stop), 1.0, 0.0)
        beyond = jnp.where((across < down) & (base + size + across < stop), 1.0, 0.0)
        prev_b, here_b = prev.astype(bf16), here.astype(bf16)
        ahead_b, beyond_b = ahead.astype(bf16), beyond.astype(bf16)
        rows = pl.ds(pl.multiple_of(tb * size, size), size)
        both = pl.ds(pl.multiple_of(tb * size, size), 2 * size)
        for half in range(2):
            lanes = slice(half * 128, half * 128 + 128)
            mixed = mw[both, lanes]
            grads = ogw[both, lanes]
            own = ogw[rows, lanes]
            out = jnp.zeros((size, size), jnp.float32)
            back = jnp.zeros((size, size), jnp.float32)
            for member in range(8):
                group = half * 8 + member
                chosen = group_of_lane == member
                band = back_circ[group]
                out = jnp.where(
                    chosen,
                    jnp.dot(
                        jnp.concatenate((band * prev_b, band * here_b), axis=1),
                        mixed,
                        preferred_element_type=jnp.float32,
                    ),
                    out,
                )
                band = circ[group]
                back = jnp.where(
                    chosen,
                    jnp.dot(
                        jnp.concatenate((band * ahead_b, band * beyond_b), axis=1),
                        grads,
                        preferred_element_type=jnp.float32,
                    ),
                    back,
                )
                outer = nt_dot(jnp.where(chosen, own, jnp.zeros_like(own)), mixed)
                tap_sum[group] += outer[:, :size] * prev + outer[:, size:] * here
            out_ref[rows, lanes] = out.astype(bf16)
            grad_ref[rows, lanes] = back.astype(bf16)
        return carried

    lax.fori_loop(0, SPAN // size, block, 0)
    mirror = jnp.where(across + down == size - 1, 1.0, 0.0)
    for group in range(CONV_GROUPS):
        upside = jnp.dot(
            mirror,
            tap_sum[group],
            precision=lax.Precision.HIGHEST,
            preferred_element_type=jnp.float32,
        )
        turned = pltpu.roll(upside, 1, 1, stride=1, stride_axis=0)
        tap_ref[group : group + 1, :] = jnp.sum(turned, axis=0, keepdims=True)


def return_kernel(
    dq, dk, dv, out, back, taps, dq_o, dk_o, dv_o, out_o, back_o, taps_o,
    slots, total, send_sem, recv_sem, zsend_sem, zrecv_sem, tap_send, tap_recv,
):
    z, p = place_in_slice()
    greet(z, p)
    shares = []
    for step in range(1, PLANES):
        copy = pltpu.make_async_remote_copy(
            src_ref=taps,
            dst_ref=slots.at[step - 1],
            send_sem=zsend_sem.at[step - 1],
            recv_sem=zrecv_sem.at[step - 1],
            device_id=device_of(lax.rem(z + step, PLANES), p),
            device_id_type=MESH,
        )
        copy.start()
        shares.append(copy)

    def send(slot, src, dst, width, block):
        mine = dst.at[:, pl.ds(pl.multiple_of(block(p) * width, width), width)]

        def rows(r):
            return src.at[pl.ds(pl.multiple_of(r * ROWS, ROWS), ROWS), :]

        pltpu.make_async_copy(rows(p), mine, recv_sem.at[slot]).start()

        def step(i, carried):
            r = lax.rem(p + i, PLANE)
            pltpu.make_async_remote_copy(
                src_ref=rows(r),
                dst_ref=mine,
                send_sem=send_sem.at[slot],
                recv_sem=recv_sem.at[slot],
                device_id=device_of(z, r),
                device_id_type=MESH,
            ).start()
            return carried

        lax.fori_loop(1, PLANE, step, 0)

    head = lambda r: r
    send(0, out, out_o, CONV_WIDTH, conv_block)
    send(1, back, back_o, CONV_WIDTH, conv_block)
    send(2, dq, dq_o, HEAD_DIM, head)
    send(3, dk, dk_o, HEAD_DIM, head)
    send(4, dv, dv_o, HEAD_DIM, head)
    for copy in shares:
        copy.wait()
    total[...] = taps[...] + slots[0] + slots[1] + slots[2]
    mine = taps_o.at[pl.ds(pl.multiple_of(lax.div(p, 4) * CONV_GROUPS, CONV_GROUPS), CONV_GROUPS), :]
    pltpu.make_async_copy(total, mine, tap_recv).start()

    def tell(i, carried):
        pltpu.make_async_remote_copy(
            src_ref=total,
            dst_ref=mine,
            send_sem=tap_send,
            recv_sem=tap_recv,
            device_id=device_of(z, lax.rem(p + 4 * i, PLANE)),
            device_id_type=MESH,
        ).start()
        return carried

    lax.fori_loop(1, PLANE // 4, tell, 0)
    for slot, (src, dst) in enumerate(
        ((out, out_o), (back, back_o), (dq, dq_o), (dk, dk_o), (dv, dv_o))
    ):
        wait_bytes(dst, recv_sem.at[slot])
        wait_bytes(src.at[pl.ds(0, SPAN - ROWS), :], send_sem.at[slot])
    wait_bytes(taps_o, tap_recv)
    wait_bytes(taps_o.at[pl.ds(0, FILTER_LEN - CONV_GROUPS), :], tap_send)


def hand_back(dq, dk, dv, out, back, taps):
    bf16 = jnp.bfloat16
    any_space = pl.BlockSpec(memory_space=pl.ANY)
    attn = jax.ShapeDtypeStruct((ROWS, PLANE * HEAD_DIM), bf16)
    conv = jax.ShapeDtypeStruct((ROWS, PLANE * CONV_WIDTH), bf16)
    dma = pltpu.SemaphoreType.DMA
    return pl.pallas_call(
        return_kernel,
        out_shape=(
            attn, attn, attn, conv, conv, jax.ShapeDtypeStruct((128, FILTER_LEN), jnp.float32),
        ),
        in_specs=[any_space] * 5 + [pl.BlockSpec(memory_space=pltpu.VMEM)],
        out_specs=(any_space,) * 6,
        scratch_shapes=[
            pltpu.VMEM((PLANES - 1, CONV_GROUPS, FILTER_LEN), jnp.float32),
            pltpu.VMEM((CONV_GROUPS, FILTER_LEN), jnp.float32),
            dma((5,)), dma((5,)), dma((3,)), dma((3,)), dma, dma,
        ],
        compiler_params=pltpu.CompilerParams(collective_id=1, has_side_effects=True),
        name="hand_back",
    )(dq, dk, dv, out, back, taps)


def call_local(kernel, name, out_shape, scratch, flops, *operands):
    vmem = pl.BlockSpec(memory_space=pltpu.VMEM)
    moved = sum(x.size * x.dtype.itemsize for x in operands)
    return pl.pallas_call(
        kernel,
        out_shape=out_shape,
        in_specs=[pl.BlockSpec(memory_space=pltpu.SMEM)] + [vmem] * (len(operands) - 1),
        out_specs=jax.tree.map(lambda _: vmem, out_shape),
        scratch_shapes=scratch,
        compiler_params=pltpu.CompilerParams(vmem_limit_bytes=VMEM_LIMIT),
        cost_estimate=pl.CostEstimate(flops=flops, bytes_accessed=moved, transcendentals=0),
        name=name,
    )(*operands)


def body(
    attn_query, attn_key, attn_value, attn_output, attn_grad_out,
    conv_query, conv_key, conv_value, conv_grad_out, conv_filter, doc_lengths,
):
    f32, bf16 = jnp.float32, jnp.bfloat16
    mixed = (conv_key.astype(f32) * conv_value.astype(f32)).astype(bf16)
    out_grad = (conv_grad_out.astype(f32) * conv_query.astype(f32)).astype(bf16)
    qw, kw, vw, ow, gw, mw, ogw = spread(
        attn_query, attn_key, attn_value, attn_output, attn_grad_out, mixed, out_grad
    )
    shape = jax.ShapeDtypeStruct
    own_stats = call_local(
        stats_kernel, "stats", shape((NEAR, 8, TILE), f32), [], 10**9, doc_lengths, qw, kw, gw, ow
    )
    seq_count = PLANE // 4 * PLANES

    def from_later(block, planes):
        shift = planes * (PLANE // 4)
        return lax.ppermute(
            block, "seq", [(i, (i - shift) % seq_count) for i in range(seq_count)]
        )

    near_stats = from_later(own_stats, 1)
    far_stats = from_later(own_stats[:1], 2)
    _, p = place_in_slice()
    taps = lax.dynamic_slice_in_dim(
        conv_filter, lax.div(p, 4) * CONV_GROUPS, CONV_GROUPS, 0
    ).astype(f32)
    flip = lambda rows: jnp.roll(rows[:, ::-1], 1, axis=1)
    square = (CONV_GROUPS, FILTER_LEN, FILTER_LEN)
    out, back, tap_grad = call_local(
        conv_kernel,
        "conv",
        (
            shape((SPAN, CONV_WIDTH), bf16),
            shape((SPAN, CONV_WIDTH), bf16),
            shape((CONV_GROUPS, FILTER_LEN), f32),
        ),
        [pltpu.VMEM(square, bf16), pltpu.VMEM(square, bf16), pltpu.VMEM(square, f32)],
        4 * 10**9,
        doc_lengths, taps, flip(taps), mw, ogw,
    )
    attn = shape((SPAN, HEAD_DIM), bf16)
    dq, dk, dv = call_local(
        grads_kernel,
        "grads",
        (attn, attn, attn),
        [
            pltpu.VMEM((NEAR + REACH, 8, TILE), f32),
            pltpu.VMEM((SPAN, HEAD_DIM), f32),
            pltpu.VMEM((SPAN, HEAD_DIM), f32),
            pltpu.VMEM((HEAD_DIM, TILE), f32),
        ],
        3 * 10**9,
        doc_lengths, qw, kw, vw, gw, own_stats, near_stats, far_stats,
    )
    dq, dk, dv, out, back, filter_grad = hand_back(dq, dk, dv, out, back, flip(tap_grad))
    back = back.astype(f32)
    return (
        dq,
        dk,
        dv,
        (conv_grad_out.astype(f32) * out.astype(f32)).astype(bf16),
        (back * conv_value.astype(f32)).astype(bf16),
        (back * conv_key.astype(f32)).astype(bf16),
        filter_grad,
    )


def solution(mesh):
    rows = P(("seq", "ch"), None)
    return jax.shard_map(
        body,
        mesh=mesh,
        in_specs=(rows,) * 9 + (P("ch", None), P()),
        out_specs=(rows,) * 6 + (P("ch", None),),
        check_vma=False,
    )
```

```python
import math

import jax
import jax.numpy as jnp
from jax import lax
from jax.experimental import pallas as pl
from jax.experimental.pallas import tpu as pltpu
from jax.sharding import PartitionSpec as P

MESH = pl.DeviceIdType.MESH
HEAD_DIM = 128
FILTER_LEN = 128
DOCS = 12
PLANE = 32
PLANES = 4
ROWS = 32
SPAN = PLANE * ROWS
TILE = 256
NEAR = SPAN // TILE
REACH = 5
WINDOW = SPAN + REACH * TILE
CONV_WIDTH = 256
CONV_GROUPS = 16
LOG2_SCALE = math.log2(math.e) / math.sqrt(HEAD_DIM)
SCALE = 1.0 / math.sqrt(HEAD_DIM)
NEG_FILL = -1e30
VMEM_LIMIT = 60 * 1024 * 1024


def place_in_slice():
    me = lax.axis_index("seq") * 4 + lax.axis_index("ch")
    return lax.div(me, PLANE), lax.rem(me, PLANE)


def device_of(z, p):
    return (z * (PLANE // 4) + lax.div(p, 4), lax.rem(p, 4))


def conv_block(p):
    return lax.rem(p, 4) * (PLANE // 4) + lax.div(p, 4)


def greet(z, p):
    barrier = pltpu.get_barrier_semaphore()

    def hello(k, carried):
        pl.semaphore_signal(
            barrier, inc=1, device_id=device_of(z, lax.rem(p + k, PLANE)), device_id_type=MESH
        )
        return carried

    lax.fori_loop(1, PLANE, hello, 0)
    for step in range(1, PLANES):
        pl.semaphore_signal(
            barrier, inc=1, device_id=device_of(lax.rem(z + step, PLANES), p), device_id_type=MESH
        )
    pl.semaphore_wait(barrier, PLANE - 1 + PLANES - 1)


def wait_bytes(ref, sem):
    pltpu.make_async_copy(ref, ref, sem).wait()


def doc_ends(len_ref):
    ends = []
    total = jnp.int32(0)
    for d in range(DOCS):
        total = total + len_ref[d]
        ends.append(total)
    return ends


def doc_start(ends, pos):
    start = jnp.zeros_like(pos)
    for end in ends:
        start = jnp.maximum(start, jnp.where(end <= pos, end, 0))
    return start


def doc_stop(ends, pos):
    stop = jnp.full_like(pos, ends[-1])
    for end in ends:
        stop = jnp.minimum(stop, jnp.where(end > pos, end, ends[-1]))
    return stop


def nt_dot(a, b):
    return lax.dot_general(a, b, (((1,), (1,)), ((), ())), preferred_element_type=jnp.float32)


def tile_rows(ref, i):
    return ref[pl.ds(pl.multiple_of(i * TILE, TILE), TILE), :]


def row_positions(base):
    return base + lax.broadcasted_iota(jnp.int32, (1, TILE), 1)


def first_tile(ends, z, q_base):
    start = doc_start(ends, q_base)
    return lax.div(start - (z * SPAN - REACH * TILE), TILE)


def seen_before(z, kb, starts):
    k_pos = z * SPAN - REACH * TILE + kb * TILE + lax.broadcasted_iota(jnp.int32, (TILE, TILE), 0)
    return k_pos >= starts


def seen_diagonal(z, kb, starts):
    below = lax.broadcasted_iota(jnp.int32, (TILE, TILE), 0) <= lax.broadcasted_iota(
        jnp.int32, (TILE, TILE), 1
    )
    return seen_before(z, kb, starts) & below


def gather_kernel(
    len_ref, q, k, v, o, g, cq, ck, cv, cg, filt,
    kv_out, qg_out, stats_out, back_out, taps_out,
    kv_in, qg_in, o_in, conv_in, pair, delta_in, delta, kv, qg, conv, result, circ, back_circ,
    tap_sum, taps, stats, running,
    load_sem, send_sem, recv_sem, zsend_sem, zrecv_sem, out_sem,
):
    z, p = place_in_slice()
    ends = doc_ends(len_ref)
    f32, bf16 = jnp.float32, jnp.bfloat16
    loads = []
    for i, (src, dst) in enumerate(
        (
            (k, kv_in.at[0]), (v, kv_in.at[1]), (q, qg_in.at[0]), (g, qg_in.at[1]), (o, o_in),
            (ck, conv_in.at[0]), (cv, conv_in.at[1]), (cg, conv_in.at[2]), (cq, conv_in.at[3]),
        )
    ):
        copy = pltpu.make_async_copy(src, dst, load_sem.at[i])
        copy.start()
        loads.append(copy)
    greet(z, p)

    def send(slot, take, give):
        pltpu.make_async_copy(take(p), give, recv_sem.at[slot]).start()

        def step(i, carried):
            r = lax.rem(p + i, PLANE)
            pltpu.make_async_remote_copy(
                src_ref=take(r),
                dst_ref=give,
                send_sem=send_sem.at[slot],
                recv_sem=recv_sem.at[slot],
                device_id=device_of(z, r),
                device_id_type=MESH,
            ).start()
            return carried

        lax.fori_loop(1, PLANE, step, 0)

    hops = {}

    def hop(slot, src, dst, step):
        copy = pltpu.make_async_remote_copy(
            src_ref=src,
            dst_ref=dst,
            send_sem=zsend_sem.at[slot],
            recv_sem=zrecv_sem.at[slot],
            device_id=device_of(lax.rem(z + step, PLANES), p),
            device_id_type=MESH,
        )
        copy.start()
        hops[slot] = copy

    def head_columns(ref):
        return lambda r: ref.at[:, :, pl.ds(pl.multiple_of(r * HEAD_DIM, HEAD_DIM), HEAD_DIM)]

    def conv_columns(ref, half):
        return lambda r: ref.at[
            :, :, pl.ds(pl.multiple_of(conv_block(r) * CONV_WIDTH + half * 128, 128), 128)
        ]

    def my_rows(base):
        return pl.ds(pl.multiple_of(base + p * ROWS, ROWS), ROWS)

    back = REACH * TILE
    size = FILTER_LEN
    loads[0].wait()
    loads[1].wait()
    send(0, head_columns(kv_in), kv.at[:, my_rows(back), :])
    loads[2].wait()
    loads[3].wait()
    send(1, head_columns(qg_in), qg.at[:, my_rows(0), :])
    for i in (5, 6, 7, 8):
        loads[i].wait()

    def products(i, carried):
        lanes = pl.ds(pl.multiple_of(i * 512, 512), 512)
        pair[0, :, lanes] = (
            conv_in[0, :, lanes].astype(f32) * conv_in[1, :, lanes].astype(f32)
        ).astype(bf16)
        pair[1, :, lanes] = (
            conv_in[2, :, lanes].astype(f32) * conv_in[3, :, lanes].astype(f32)
        ).astype(bf16)
        return carried

    lax.fori_loop(0, PLANE * CONV_WIDTH // 512, products, 0)
    loads[4].wait()

    def deltas(h, carried):
        lanes = pl.ds(pl.multiple_of(h * HEAD_DIM, HEAD_DIM), HEAD_DIM)
        terms = qg_in[1, :, lanes].astype(f32) * o_in[:, lanes].astype(f32)
        padded = jnp.concatenate((terms, jnp.zeros((HEAD_DIM - ROWS, HEAD_DIM), f32)), axis=0)
        delta_in[h] = jnp.sum(padded.T, axis=0, keepdims=True)
        return carried

    lax.fori_loop(0, PLANE, deltas, 0)
    send(2, conv_columns(pair, 0), conv.at[0, :, my_rows(size), :])
    send(3, lambda r: delta_in.at[r], delta.at[p])
    send(4, conv_columns(pair, 1), conv.at[1, :, my_rows(size), :])

    down = lax.broadcasted_iota(jnp.int32, (size, size), 0)
    across = lax.broadcasted_iota(jnp.int32, (size, size), 1)
    mirror = jnp.where(lax.rem(across + down, size) == 0, 1.0, 0.0)
    own_taps = filt[
        pl.ds(pl.multiple_of(lax.div(p, 4) * CONV_GROUPS, CONV_GROUPS), CONV_GROUPS), :
    ]
    flipped = jnp.dot(own_taps, mirror.astype(bf16), preferred_element_type=f32)
    own_taps = own_taps.astype(f32)
    for group in range(CONV_GROUPS):
        for src, dst in ((own_taps, circ), (flipped, back_circ)):
            row = jnp.broadcast_to(src[group : group + 1, :], (size, size))
            dst[group] = pltpu.roll(row, 0, 1, stride=1, stride_axis=0).astype(bf16)
    tap_sum[...] = jnp.zeros_like(tap_sum)
    stats[0:NEAR] = jnp.zeros((NEAR, 8, TILE), f32)

    wait_bytes(kv.at[:, pl.ds(back, SPAN), :], recv_sem.at[0])
    hop(0, kv.at[:, pl.ds(back, SPAN), :], kv.at[:, pl.ds(TILE, SPAN), :], 1)
    hop(1, kv.at[:, pl.ds(SPAN + back - TILE, TILE), :], kv.at[:, pl.ds(0, TILE), :], 2)
    wait_bytes(qg.at[:, pl.ds(0, SPAN), :], recv_sem.at[1])
    hop(2, qg.at[:, pl.ds(0, SPAN), :], qg.at[:, pl.ds(SPAN, SPAN), :], 3)
    hop(3, qg.at[:, pl.ds(0, TILE), :], qg.at[:, pl.ds(2 * SPAN, TILE), :], 2)

    def scores(qi, kb, seen):
        starts = doc_start(ends, row_positions(z * SPAN + qi * TILE))
        s = nt_dot(tile_rows(kv.at[0], kb), tile_rows(qg.at[0], qi)) * LOG2_SCALE
        return jnp.where(seen(z, kb, starts), s, NEG_FILL)

    def extend(qi, kb, state):
        top, total = state
        s = scores(qi, kb, seen_before)
        new_top = jnp.maximum(top, jnp.max(s, axis=0, keepdims=True))
        total = total * jnp.exp2(top - new_top) + jnp.sum(
            jnp.exp2(s - new_top), axis=0, keepdims=True
        )
        return new_top, total

    def own_tiles(qi, carried):
        s = scores(qi, qi + REACH, seen_diagonal)
        top = jnp.max(s, axis=0, keepdims=True)
        total = jnp.sum(jnp.exp2(s - top), axis=0, keepdims=True)
        top, total = lax.fori_loop(
            REACH, REACH + qi, lambda kb, state: extend(qi, kb, state), (top, total)
        )
        running[qi, 0:1, :] = top
        running[qi, 1:2, :] = total
        return carried

    def earlier_tiles(qi, carried):
        top, total = lax.fori_loop(
            qi,
            REACH,
            lambda kb, state: extend(qi, kb, state),
            (running[qi, 0:1, :], running[qi, 1:2, :]),
        )
        stats[qi, 0:1, :] = top + jnp.log2(total)
        for side in range(2):
            row = jnp.zeros((1, HEAD_DIM), f32)
            for part in range(4):
                row = row + pltpu.roll(delta[qi * 8 + side * 4 + part], part * ROWS, 1)
            stats[qi, 1:2, side * HEAD_DIM : (side + 1) * HEAD_DIM] = row
        return carried

    def conv_rows(half, kind, start, count):
        return conv.at[half, kind, pl.ds(start, count), :]

    def halo(half):
        wait_bytes(conv.at[half, :, pl.ds(size, SPAN), :], recv_sem.at[2 + 2 * half])
        hop(4 + half, conv_rows(half, 0, SPAN, size), conv_rows(half, 0, 0, size), 1)
        hop(6 + half, conv_rows(half, 1, size, size), conv_rows(half, 1, SPAN + size, size), 3)

    group_of_lane = lax.div(across, 16)

    def conv_tile(half, tb):
        base = z * SPAN + tb * size
        positions = base + lax.broadcasted_iota(jnp.int32, (1, size), 1)

        def as_column(row):
            return jnp.broadcast_to(row.astype(f32), (size, size)).T.astype(jnp.int32)

        start = as_column(doc_start(ends, positions))
        stop = as_column(doc_stop(ends, positions))
        prev = jnp.where((across > down) & (base - size + across >= start), 1.0, 0.0)
        here = jnp.where((across <= down) & (base + across >= start), 1.0, 0.0)
        ahead = jnp.where((across >= down) & (base + across < stop), 1.0, 0.0)
        beyond = jnp.where((across < down) & (base + size + across < stop), 1.0, 0.0)
        prev_b, here_b = prev.astype(bf16), here.astype(bf16)
        ahead_b, beyond_b = ahead.astype(bf16), beyond.astype(bf16)
        rows = pl.ds(pl.multiple_of(tb * size, size), size)
        here_rows = pl.ds(pl.multiple_of(tb * size + size, size), size)
        mixed = conv[half, 0, pl.ds(pl.multiple_of(tb * size, size), 2 * size), :]
        grads = conv[half, 1, pl.ds(pl.multiple_of(tb * size + size, size), 2 * size), :]
        own = conv[half, 1, here_rows, :]
        out = jnp.zeros((size, size), f32)
        inner = jnp.zeros((size, size), f32)
        for member in range(8):
            group = half * 8 + member
            chosen = group_of_lane == member
            band = back_circ[group]
            out = jnp.where(
                chosen,
                jnp.dot(
                    jnp.concatenate((band * prev_b, band * here_b), axis=1),
                    mixed,
                    preferred_element_type=f32,
                ),
                out,
            )
            band = circ[group]
            inner = jnp.where(
                chosen,
                jnp.dot(
                    jnp.concatenate((band * ahead_b, band * beyond_b), axis=1),
                    grads,
                    preferred_element_type=f32,
                ),
                inner,
            )
            outer = nt_dot(jnp.where(chosen, own, jnp.zeros_like(own)), mixed)
            tap_sum[group] += outer[:, :size] * prev + outer[:, size:] * here
        result[half, 0, rows, :] = out.astype(bf16)
        result[half, 1, rows, :] = inner.astype(bf16)

    def conv_back(half, tb):
        columns = pl.ds(pl.multiple_of(conv_block(p) * CONV_WIDTH + half * 128, 128), 128)
        mine = back_out.at[:, :, columns]

        def one(i, carried):
            r = tb * 4 + i
            rows = result.at[half, :, pl.ds(pl.multiple_of(r * ROWS, ROWS), ROWS), :]

            @pl.when(r == p)
            def _():
                pltpu.make_async_copy(rows, mine, recv_sem.at[5]).start()

            @pl.when(r != p)
            def _():
                pltpu.make_async_remote_copy(
                    src_ref=rows,
                    dst_ref=mine,
                    send_sem=send_sem.at[5],
                    recv_sem=recv_sem.at[5],
                    device_id=device_of(z, r),
                    device_id_type=MESH,
                ).start()

            return carried

        lax.fori_loop(0, 4, one, 0)

    def conv_half(half):
        turn = lax.div(p, 4)

        def inner_tile(i, carried):
            tb = 1 + lax.rem(i + turn, 6)
            conv_tile(half, tb)
            conv_back(half, tb)
            return carried

        def edge_tile(i, carried):
            tb = 7 * lax.rem(i + turn, 2)
            conv_tile(half, tb)
            conv_back(half, tb)
            return carried

        lax.fori_loop(0, 6, inner_tile, 0)
        hops[4 + half].wait()
        hops[6 + half].wait()
        lax.fori_loop(0, 2, edge_tile, 0)

    lax.fori_loop(0, NEAR, own_tiles, 0)
    wait_bytes(delta, recv_sem.at[3])
    halo(0)
    conv_half(0)
    halo(1)
    hops[0].wait()
    hops[1].wait()
    kv_copy = pltpu.make_async_copy(kv, kv_out, out_sem.at[0])
    kv_copy.start()
    lax.fori_loop(0, NEAR, earlier_tiles, 0)
    conv_half(1)
    hop(8, stats.at[pl.ds(0, NEAR)], stats.at[pl.ds(NEAR, NEAR)], 3)
    hop(9, stats.at[pl.ds(0, 1)], stats.at[pl.ds(2 * NEAR, 1)], 2)
    hops[2].wait()
    hops[3].wait()
    qg_copy = pltpu.make_async_copy(qg, qg_out, out_sem.at[1])
    qg_copy.start()
    upside_down = jnp.where(across + down == size - 1, 1.0, 0.0)
    for group in range(CONV_GROUPS):
        upside = jnp.dot(
            upside_down, tap_sum[group], precision=lax.Precision.HIGHEST, preferred_element_type=f32
        )
        turned = pltpu.roll(upside, 1, 1, stride=1, stride_axis=0)
        taps[0, group : group + 1, :] = jnp.sum(turned, axis=0, keepdims=True)
    hops[8].wait()
    hops[9].wait()
    stats_copy = pltpu.make_async_copy(stats, stats_out, out_sem.at[2])
    stats_copy.start()
    for step in range(1, PLANES):
        hop(9 + step, taps.at[0], taps.at[step], step)
    for step in range(1, PLANES):
        hops[9 + step].wait()
    taps_copy = pltpu.make_async_copy(taps, taps_out, out_sem.at[3])
    taps_copy.start()
    most = PLANE - 1
    wait_bytes(kv.at[:, pl.ds(0, most * ROWS), :], send_sem.at[0])
    wait_bytes(qg.at[:, pl.ds(0, most * ROWS), :], send_sem.at[1])
    wait_bytes(conv.at[0, :, pl.ds(0, most * ROWS), :], send_sem.at[2])
    wait_bytes(delta.at[pl.ds(0, most)], send_sem.at[3])
    wait_bytes(conv.at[1, :, pl.ds(0, most * ROWS), :], send_sem.at[4])
    wait_bytes(back_out.at[:, :, pl.ds(0, most * CONV_WIDTH)], send_sem.at[5])
    wait_bytes(back_out, recv_sem.at[5])
    for copy in (kv_copy, qg_copy, stats_copy, taps_copy):
        copy.wait()


def gather(doc_lengths, q, k, v, o, g, cq, ck, cv, cg, filt):
    f32, bf16 = jnp.float32, jnp.bfloat16
    any_space = pl.BlockSpec(memory_space=pl.ANY)
    shape = jax.ShapeDtypeStruct
    vmem, dma = pltpu.VMEM, pltpu.SemaphoreType.DMA
    square = (CONV_GROUPS, FILTER_LEN, FILTER_LEN)
    features, channels = PLANE * HEAD_DIM, PLANE * CONV_WIDTH
    return pl.pallas_call(
        gather_kernel,
        out_shape=(
            shape((2, WINDOW, HEAD_DIM), bf16),
            shape((2, WINDOW, HEAD_DIM), bf16),
            shape((NEAR + REACH, 8, TILE), f32),
            shape((2, ROWS, channels), bf16),
            shape((PLANES, CONV_GROUPS, FILTER_LEN), f32),
        ),
        in_specs=[pl.BlockSpec(memory_space=pltpu.SMEM)]
        + [any_space] * 9
        + [pl.BlockSpec(memory_space=pltpu.VMEM)],
        out_specs=(any_space,) * 5,
        scratch_shapes=[
            vmem((2, ROWS, features), bf16),
            vmem((2, ROWS, features), bf16),
            vmem((ROWS, features), bf16),
            vmem((4, ROWS, channels), bf16),
            vmem((2, ROWS, channels), bf16),
            vmem((PLANE, 1, HEAD_DIM), f32),
            vmem((PLANE, 1, HEAD_DIM), f32),
            vmem((2, WINDOW, HEAD_DIM), bf16),
            vmem((2, WINDOW, HEAD_DIM), bf16),
            vmem((2, 2, SPAN + 2 * FILTER_LEN, 128), bf16),
            vmem((2, 2, SPAN, 128), bf16),
            vmem(square, bf16),
            vmem(square, bf16),
            vmem(square, f32),
            vmem((PLANES, CONV_GROUPS, FILTER_LEN), f32),
            vmem((NEAR + REACH, 8, TILE), f32),
            vmem((NEAR, 8, TILE), f32),
            dma((9,)), dma((6,)), dma((6,)), dma((13,)), dma((13,)), dma((4,)),
        ],
        compiler_params=pltpu.CompilerParams(
            collective_id=0, has_side_effects=True, vmem_limit_bytes=VMEM_LIMIT
        ),
        name="gather",
    )(doc_lengths, q, k, v, o, g, cq, ck, cv, cg, filt)


def grads_kernel(
    len_ref, kv, qg, stats, taps, back, cg, cv, ck,
    grads_out, gcq, gck, gcv, taps_out,
    dk_sum, dv_sum, dq_sum, conv_in, conv_res, load_sem, store_sem,
):
    z, _ = place_in_slice()
    ends = doc_ends(len_ref)
    f32, bf16 = jnp.float32, jnp.bfloat16
    kw, vw, qw, gw = kv.at[0], kv.at[1], qg.at[0], qg.at[1]
    loads = [
        pltpu.make_async_copy(src, dst, load_sem.at[i])
        for i, (src, dst) in enumerate(
            (
                (back.at[0], conv_in.at[0]), (back.at[1], conv_in.at[1]),
                (cg, conv_in.at[2]), (cv, conv_in.at[3]), (ck, conv_in.at[4]),
            )
        )
    ]
    for copy in loads:
        copy.start()
    dk_sum[...] = jnp.zeros_like(dk_sum)
    dv_sum[...] = jnp.zeros_like(dv_sum)
    size = FILTER_LEN
    down = lax.broadcasted_iota(jnp.int32, (size, size), 0)
    across = lax.broadcasted_iota(jnp.int32, (size, size), 1)
    mirror = jnp.where(lax.rem(across + down, size) == 0, 1.0, 0.0)
    taps_out[...] = jnp.dot(
        (taps[0] + taps[1]) + (taps[2] + taps[3]),
        mirror,
        precision=lax.Precision.HIGHEST,
        preferred_element_type=f32,
    )

    def pair(qi, kb, starts, seen, for_query, for_key):
        query = tile_rows(qw, qi)
        grad = tile_rows(gw, qi)
        key = tile_rows(kw, kb)
        s = nt_dot(key, query) * LOG2_SCALE - stats[qi, 0:1, :]
        probs = jnp.where(seen(z, kb, starts), jnp.exp2(s), 0.0)
        grad_scores = probs * (nt_dot(tile_rows(vw, kb), grad) - stats[qi, 1:2, :])
        grad_scores = grad_scores.astype(jnp.bfloat16)
        if for_key:
            rows = pl.ds(pl.multiple_of((kb - REACH) * TILE, TILE), TILE)
            dv_sum[rows, :] += jnp.dot(
                probs.astype(jnp.bfloat16), grad, preferred_element_type=jnp.float32
            )
            dk_sum[rows, :] += jnp.dot(grad_scores, query, preferred_element_type=jnp.float32)
        if for_query:
            dq_sum[...] += lax.dot_general(
                key, grad_scores, (((0,), (0,)), ((), ())), preferred_element_type=jnp.float32
            )

    def own_tile(qi, carried):
        q_base = z * SPAN + qi * TILE
        starts = doc_start(ends, row_positions(q_base))
        first = first_tile(ends, z, q_base)
        dq_sum[...] = jnp.zeros_like(dq_sum)

        def before(kb, inner):
            pair(qi, kb, starts, seen_before, True, False)
            return inner

        def within(kb, inner):
            pair(qi, kb, starts, seen_before, True, True)
            return inner

        lax.fori_loop(first, REACH, before, 0)
        lax.fori_loop(jnp.maximum(first, REACH), REACH + qi, within, 0)
        pair(qi, REACH + qi, starts, seen_diagonal, True, True)
        rows = pl.ds(pl.multiple_of(qi * TILE, TILE), TILE)
        grads_out[0, rows, :] = (dq_sum[...].T * SCALE).astype(jnp.bfloat16)
        return carried

    lax.fori_loop(0, NEAR, own_tile, 0)
    for copy in loads:
        copy.wait()

    def gates(i, carried):
        lanes = pl.ds(pl.multiple_of(i * 512, 512), 512)
        inner = conv_in[1, :, lanes].astype(f32)
        pieces = (
            (0, conv_in[0, :, lanes].astype(f32), 2), (1, inner, 3), (2, inner, 4),
        )
        for slot, left, right in pieces:
            conv_res[slot, :, lanes] = (left * conv_in[right, :, lanes].astype(f32)).astype(bf16)
        return carried

    lax.fori_loop(0, PLANE * CONV_WIDTH // 512, gates, 0)
    stores = [
        pltpu.make_async_copy(conv_res.at[i], dst, store_sem.at[i])
        for i, dst in enumerate((gcq, gck, gcv))
    ]
    for copy in stores:
        copy.start()

    def later_tile(qi, carried):
        q_base = z * SPAN + qi * TILE
        starts = doc_start(ends, row_positions(q_base))

        def after(kb, inner):
            pair(qi, kb, starts, seen_before, False, True)
            return inner

        first = jnp.maximum(first_tile(ends, z, q_base), REACH)
        lax.fori_loop(first, REACH + NEAR, after, 0)
        return carried

    lax.fori_loop(NEAR, NEAR + REACH, later_tile, 0)
    grads_out[1] = (dk_sum[...] * SCALE).astype(jnp.bfloat16)
    grads_out[2] = dv_sum[...].astype(jnp.bfloat16)
    for copy in stores:
        copy.wait()


def local_grads(doc_lengths, kv, qg, stats, taps, back, cg, cv, ck):
    f32, bf16 = jnp.float32, jnp.bfloat16
    any_space = pl.BlockSpec(memory_space=pl.ANY)
    vmem_space = pl.BlockSpec(memory_space=pltpu.VMEM)
    shape = jax.ShapeDtypeStruct
    rows = shape(cg.shape, bf16)
    return pl.pallas_call(
        grads_kernel,
        out_shape=(
            shape((3, SPAN, HEAD_DIM), bf16),
            rows,
            rows,
            rows,
            shape((CONV_GROUPS, FILTER_LEN), f32),
        ),
        in_specs=[pl.BlockSpec(memory_space=pltpu.SMEM)] + [vmem_space] * 4 + [any_space] * 4,
        out_specs=(vmem_space, any_space, any_space, any_space, vmem_space),
        scratch_shapes=[
            pltpu.VMEM((SPAN, HEAD_DIM), f32),
            pltpu.VMEM((SPAN, HEAD_DIM), f32),
            pltpu.VMEM((HEAD_DIM, TILE), f32),
            pltpu.VMEM((5,) + cg.shape, bf16),
            pltpu.VMEM((3,) + cg.shape, bf16),
            pltpu.SemaphoreType.DMA((5,)),
            pltpu.SemaphoreType.DMA((3,)),
        ],
        compiler_params=pltpu.CompilerParams(vmem_limit_bytes=VMEM_LIMIT),
        name="grads",
    )(doc_lengths, kv, qg, stats, taps, back, cg, cv, ck)


def return_kernel(grads, taps, grads_o, taps_o, send_sem, recv_sem, tap_send, tap_recv):
    z, p = place_in_slice()
    greet(z, p)
    mine = grads_o.at[:, :, pl.ds(pl.multiple_of(p * HEAD_DIM, HEAD_DIM), HEAD_DIM)]

    def rows(r):
        return grads.at[:, pl.ds(pl.multiple_of(r * ROWS, ROWS), ROWS), :]

    pltpu.make_async_copy(rows(p), mine, recv_sem).start()
    taps_at = pl.ds(pl.multiple_of(lax.div(p, 4) * CONV_GROUPS, CONV_GROUPS), CONV_GROUPS)
    pltpu.make_async_copy(taps, taps_o.at[taps_at, :], tap_recv).start()

    def tell(i, carried):
        pltpu.make_async_remote_copy(
            src_ref=taps,
            dst_ref=taps_o.at[taps_at, :],
            send_sem=tap_send,
            recv_sem=tap_recv,
            device_id=device_of(z, lax.rem(p + 4 * i, PLANE)),
            device_id_type=MESH,
        ).start()
        return carried

    def step(i, carried):
        r = lax.rem(p + i, PLANE)
        pltpu.make_async_remote_copy(
            src_ref=rows(r),
            dst_ref=mine,
            send_sem=send_sem,
            recv_sem=recv_sem,
            device_id=device_of(z, r),
            device_id_type=MESH,
        ).start()
        return carried

    lax.fori_loop(1, PLANE, step, 0)
    lax.fori_loop(1, PLANE // 4, tell, 0)
    wait_bytes(grads_o, recv_sem)
    wait_bytes(grads.at[:, pl.ds(0, SPAN - ROWS), :], send_sem)
    wait_bytes(taps_o, tap_recv)
    wait_bytes(taps_o.at[pl.ds(0, FILTER_LEN - CONV_GROUPS), :], tap_send)


def hand_back(grads, taps):
    any_space = pl.BlockSpec(memory_space=pl.ANY)
    dma = pltpu.SemaphoreType.DMA
    return pl.pallas_call(
        return_kernel,
        out_shape=(
            jax.ShapeDtypeStruct((3, ROWS, PLANE * HEAD_DIM), jnp.bfloat16),
            jax.ShapeDtypeStruct((128, FILTER_LEN), jnp.float32),
        ),
        in_specs=[any_space] * 2,
        out_specs=(any_space,) * 2,
        scratch_shapes=[dma, dma, dma, dma],
        compiler_params=pltpu.CompilerParams(collective_id=1, has_side_effects=True),
        name="hand_back",
    )(grads, taps)


def finish_kernel(grads, taps, dq, dk, dv, taps_out):
    dq[...] = grads[0]
    dk[...] = grads[1]
    dv[...] = grads[2]
    taps_out[...] = taps[...]


def finish(grads, taps):
    vmem_space = pl.BlockSpec(memory_space=pltpu.VMEM)
    rows = jax.ShapeDtypeStruct(grads.shape[1:], grads.dtype)
    return pl.pallas_call(
        finish_kernel,
        out_shape=(rows, rows, rows, jax.ShapeDtypeStruct(taps.shape, taps.dtype)),
        in_specs=[vmem_space] * 2,
        out_specs=(vmem_space,) * 4,
        name="finish",
    )(grads, taps)


def body(
    attn_query, attn_key, attn_value, attn_output, attn_grad_out,
    conv_query, conv_key, conv_value, conv_grad_out, conv_filter, doc_lengths,
):
    kv, qg, stats, back, taps = gather(
        doc_lengths, attn_query, attn_key, attn_value, attn_output, attn_grad_out,
        conv_query, conv_key, conv_value, conv_grad_out, conv_filter,
    )
    grads, gcq, gck, gcv, taps = local_grads(
        doc_lengths, kv, qg, stats, taps, back, conv_grad_out, conv_value, conv_key
    )
    dq, dk, dv, filter_grad = finish(*hand_back(grads, taps))
    return dq, dk, dv, gcq, gck, gcv, filter_grad


def solution(mesh):
    rows = P(("seq", "ch"), None)
    return jax.shard_map(
        body,
        mesh=mesh,
        in_specs=(rows,) * 9 + (P("ch", None), P()),
        out_specs=(rows,) * 6 + (P("ch", None),),
        check_vma=False,
    )
```

```python
import math

import jax
import jax.numpy as jnp
from jax import lax
from jax.experimental import pallas as pl
from jax.experimental.pallas import tpu as pltpu
from jax.sharding import PartitionSpec as P

MESH = pl.DeviceIdType.MESH
HEAD_DIM = 128
FILTER_LEN = 128
DOCS = 12
PLANE = 32
PLANES = 4
ROWS = 32
SPAN = PLANE * ROWS
TILE = 256
NEAR = SPAN // TILE
REACH = 5
WINDOW = SPAN + REACH * TILE
CONV_WIDTH = 256
CONV_GROUPS = 16
LOG2_SCALE = math.log2(math.e) / math.sqrt(HEAD_DIM)
SCALE = 1.0 / math.sqrt(HEAD_DIM)
NEG_FILL = -1e30
VMEM_LIMIT = 60 * 1024 * 1024


def place_in_slice():
    me = lax.axis_index("seq") * 4 + lax.axis_index("ch")
    return lax.div(me, PLANE), lax.rem(me, PLANE)


def device_of(z, p):
    return (z * (PLANE // 4) + lax.div(p, 4), lax.rem(p, 4))


def conv_block(p):
    return lax.rem(p, 4) * (PLANE // 4) + lax.div(p, 4)


def partner(p, i):
    turn, member = lax.div(i, 16), lax.rem(i, 16)
    across = lax.rem(member, 4)
    down = lax.rem(lax.div(member, 4) + 3 * member, 4)
    x = lax.rem(lax.rem(lax.div(p, 2), 4) + across, 4)
    y = lax.rem(lax.div(p, 8) + down, 4)
    return y * 8 + x * 2 + lax.rem(p + turn, 2)


def greet(z, p):
    barrier = pltpu.get_barrier_semaphore()

    def hello(k, carried):
        pl.semaphore_signal(
            barrier, inc=1, device_id=device_of(z, lax.rem(p + k, PLANE)), device_id_type=MESH
        )
        return carried

    lax.fori_loop(1, PLANE, hello, 0)
    for step in range(1, PLANES):
        pl.semaphore_signal(
            barrier, inc=1, device_id=device_of(lax.rem(z + step, PLANES), p), device_id_type=MESH
        )
    pl.semaphore_wait(barrier, PLANE - 1 + PLANES - 1)


def wait_bytes(ref, sem):
    pltpu.make_async_copy(ref, ref, sem).wait()


def doc_ends(len_ref):
    ends = []
    total = jnp.int32(0)
    for d in range(DOCS):
        total = total + len_ref[d]
        ends.append(total)
    return ends


def doc_start(ends, pos):
    start = jnp.zeros_like(pos)
    for end in ends:
        start = jnp.maximum(start, jnp.where(end <= pos, end, 0))
    return start


def doc_stop(ends, pos):
    stop = jnp.full_like(pos, ends[-1])
    for end in ends:
        stop = jnp.minimum(stop, jnp.where(end > pos, end, ends[-1]))
    return stop


def nt_dot(a, b):
    return lax.dot_general(a, b, (((1,), (1,)), ((), ())), preferred_element_type=jnp.float32)


def tile_rows(ref, i):
    return ref[pl.ds(pl.multiple_of(i * TILE, TILE), TILE), :]


def row_positions(base):
    return base + lax.broadcasted_iota(jnp.int32, (1, TILE), 1)


def seen_before(z, kb, starts):
    k_pos = z * SPAN - REACH * TILE + kb * TILE + lax.broadcasted_iota(jnp.int32, (TILE, TILE), 0)
    return k_pos >= starts


def seen_diagonal(z, kb, starts):
    below = lax.broadcasted_iota(jnp.int32, (TILE, TILE), 0) <= lax.broadcasted_iota(
        jnp.int32, (TILE, TILE), 1
    )
    return seen_before(z, kb, starts) & below


def exchange_kernel(
    len_ref, q, k, v, o, g, cq, ck, cv, cg, filt,
    grads_out, back_out, taps_out,
    kv_in, qg_in, o_in, conv_in, pair, delta_in, delta, kv, qg, conv, result, circ, back_circ,
    tap_sum, folded, taps, stats, running, saved, tops, dk_sum, dv_sum, dq_sum, grads, tap_total,
    load_sem, send_sem, recv_sem, zsend_sem, zrecv_sem,
):
    z, p = place_in_slice()
    ends = doc_ends(len_ref)
    f32, bf16 = jnp.float32, jnp.bfloat16
    loads = []
    for i, (src, dst) in enumerate(
        (
            (k, kv_in.at[0]), (v, kv_in.at[1]), (q, qg_in.at[0]), (g, qg_in.at[1]), (o, o_in),
            (ck, conv_in.at[0]), (cv, conv_in.at[1]), (cg, conv_in.at[2]), (cq, conv_in.at[3]),
        )
    ):
        copy = pltpu.make_async_copy(src, dst, load_sem.at[i])
        copy.start()
        loads.append(copy)
    greet(z, p)

    def send(slot, take, give):
        pltpu.make_async_copy(take(p), give, recv_sem.at[slot]).start()

        def step(i, carried):
            r = partner(p, i)
            pltpu.make_async_remote_copy(
                src_ref=take(r),
                dst_ref=give,
                send_sem=send_sem.at[slot],
                recv_sem=recv_sem.at[slot],
                device_id=device_of(z, r),
                device_id_type=MESH,
            ).start()
            return carried

        lax.fori_loop(1, PLANE, step, 0)

    hops = {}

    def hop(slot, src, dst, step):
        copy = pltpu.make_async_remote_copy(
            src_ref=src,
            dst_ref=dst,
            send_sem=zsend_sem.at[slot],
            recv_sem=zrecv_sem.at[slot],
            device_id=device_of(lax.rem(z + step, PLANES), p),
            device_id_type=MESH,
        )
        copy.start()
        hops[slot] = copy

    def head_columns(ref):
        return lambda r: ref.at[:, :, pl.ds(pl.multiple_of(r * HEAD_DIM, HEAD_DIM), HEAD_DIM)]

    def conv_columns(ref, half):
        return lambda r: ref.at[
            :, :, pl.ds(pl.multiple_of(conv_block(r) * CONV_WIDTH + half * 128, 128), 128)
        ]

    def my_rows(base):
        return pl.ds(pl.multiple_of(base + p * ROWS, ROWS), ROWS)

    back = REACH * TILE
    size = FILTER_LEN
    loads[0].wait()
    loads[1].wait()
    send(0, head_columns(kv_in), kv.at[:, my_rows(back), :])
    loads[2].wait()
    loads[3].wait()
    send(1, head_columns(qg_in), qg.at[:, my_rows(0), :])
    for i in (5, 6, 7, 8):
        loads[i].wait()

    def products(i, carried):
        lanes = pl.ds(pl.multiple_of(i * 512, 512), 512)
        pair[0, :, lanes] = (
            conv_in[0, :, lanes].astype(f32) * conv_in[1, :, lanes].astype(f32)
        ).astype(bf16)
        pair[1, :, lanes] = (
            conv_in[2, :, lanes].astype(f32) * conv_in[3, :, lanes].astype(f32)
        ).astype(bf16)
        return carried

    lax.fori_loop(0, PLANE * CONV_WIDTH // 512, products, 0)
    loads[4].wait()

    def deltas(h, carried):
        lanes = pl.ds(pl.multiple_of(h * HEAD_DIM, HEAD_DIM), HEAD_DIM)
        terms = qg_in[1, :, lanes].astype(f32) * o_in[:, lanes].astype(f32)
        padded = jnp.concatenate((terms, jnp.zeros((HEAD_DIM - ROWS, HEAD_DIM), f32)), axis=0)
        delta_in[h] = jnp.sum(padded.T, axis=0, keepdims=True)
        return carried

    lax.fori_loop(0, PLANE, deltas, 0)
    send(2, conv_columns(pair, 0), conv.at[0, :, my_rows(size), :])
    send(3, lambda r: delta_in.at[r], delta.at[p])
    send(4, conv_columns(pair, 1), conv.at[1, :, my_rows(size), :])

    down = lax.broadcasted_iota(jnp.int32, (size, size), 0)
    across = lax.broadcasted_iota(jnp.int32, (size, size), 1)
    mirror = jnp.where(lax.rem(across + down, size) == 0, 1.0, 0.0)
    own_taps = filt[
        pl.ds(pl.multiple_of(lax.div(p, 4) * CONV_GROUPS, CONV_GROUPS), CONV_GROUPS), :
    ]
    flipped = jnp.dot(own_taps, mirror.astype(bf16), preferred_element_type=f32)
    own_taps = own_taps.astype(f32)
    for group in range(CONV_GROUPS):
        for src, dst in ((own_taps, circ), (flipped, back_circ)):
            row = jnp.broadcast_to(src[group : group + 1, :], (size, size))
            dst[group] = pltpu.roll(row, 0, 1, stride=1, stride_axis=0).astype(bf16)
    tap_sum[...] = jnp.zeros_like(tap_sum)
    stats[0:NEAR] = jnp.zeros((NEAR, 8, TILE), f32)

    wait_bytes(kv.at[:, pl.ds(back, SPAN), :], recv_sem.at[0])
    hop(0, kv.at[:, pl.ds(back, SPAN), :], kv.at[:, pl.ds(TILE, SPAN), :], 1)
    hop(1, kv.at[:, pl.ds(SPAN + back - TILE, TILE), :], kv.at[:, pl.ds(0, TILE), :], 2)
    wait_bytes(qg.at[:, pl.ds(0, SPAN), :], recv_sem.at[1])
    hop(2, qg.at[:, pl.ds(0, SPAN), :], qg.at[:, pl.ds(SPAN, SPAN), :], 3)
    hop(3, qg.at[:, pl.ds(0, TILE), :], qg.at[:, pl.ds(2 * SPAN, TILE), :], 2)

    def scores(qi, kb, seen):
        starts = doc_start(ends, row_positions(z * SPAN + qi * TILE))
        s = nt_dot(tile_rows(kv.at[0], kb), tile_rows(qg.at[0], qi)) * LOG2_SCALE
        return jnp.where(seen(z, kb, starts), s, NEG_FILL)

    def keep(qi, kb, s, top):
        slot = qi * REACH + kb
        weights = jnp.exp2(s - top)
        saved[slot] = weights
        tops[slot, 0:1, :] = top
        return jnp.sum(weights, axis=0, keepdims=True)

    def extend(qi, kb, state):
        top, total = state
        s = scores(qi, kb, seen_before)
        new_top = jnp.maximum(top, jnp.max(s, axis=0, keepdims=True))
        total = total * jnp.exp2(top - new_top) + keep(qi, kb, s, new_top)
        return new_top, total

    def own_tiles(qi, carried):
        s = scores(qi, qi + REACH, seen_diagonal)
        top = jnp.max(s, axis=0, keepdims=True)
        total = keep(qi, qi + REACH, s, top)
        top, total = lax.fori_loop(
            REACH, REACH + qi, lambda kb, state: extend(qi, kb, state), (top, total)
        )
        running[qi, 0:1, :] = top
        running[qi, 1:2, :] = total
        return carried

    def earlier_tiles(qi, carried):
        top, total = lax.fori_loop(
            qi,
            REACH,
            lambda kb, state: extend(qi, kb, state),
            (running[qi, 0:1, :], running[qi, 1:2, :]),
        )
        stats[qi, 0:1, :] = top + jnp.log2(total)
        for side in range(2):
            row = jnp.zeros((1, HEAD_DIM), f32)
            for part in range(4):
                row = row + pltpu.roll(delta[qi * 8 + side * 4 + part], part * ROWS, 1)
            stats[qi, 1:2, side * HEAD_DIM : (side + 1) * HEAD_DIM] = row
        return carried

    def conv_rows(half, kind, start, count):
        return conv.at[half, kind, pl.ds(start, count), :]

    def halo(half):
        wait_bytes(conv.at[half, :, pl.ds(size, SPAN), :], recv_sem.at[2 + 2 * half])
        hop(4 + half, conv_rows(half, 0, SPAN, size), conv_rows(half, 0, 0, size), 1)
        hop(6 + half, conv_rows(half, 1, size, size), conv_rows(half, 1, SPAN + size, size), 3)

    group_of_lane = lax.div(across, 16)

    def conv_tile(half, tb):
        base = z * SPAN + tb * size
        positions = base + lax.broadcasted_iota(jnp.int32, (1, size), 1)

        def as_column(row):
            return jnp.broadcast_to(row.astype(f32), (size, size)).T.astype(jnp.int32)

        start = as_column(doc_start(ends, positions))
        stop = as_column(doc_stop(ends, positions))
        prev = jnp.where((across > down) & (base - size + across >= start), 1.0, 0.0)
        here = jnp.where((across <= down) & (base + across >= start), 1.0, 0.0)
        ahead = jnp.where((across >= down) & (base + across < stop), 1.0, 0.0)
        beyond = jnp.where((across < down) & (base + size + across < stop), 1.0, 0.0)
        prev_b, here_b = prev.astype(bf16), here.astype(bf16)
        ahead_b, beyond_b = ahead.astype(bf16), beyond.astype(bf16)
        rows = pl.ds(pl.multiple_of(tb * size, size), size)
        here_rows = pl.ds(pl.multiple_of(tb * size + size, size), size)
        mixed = conv[half, 0, pl.ds(pl.multiple_of(tb * size, size), 2 * size), :]
        grads = conv[half, 1, pl.ds(pl.multiple_of(tb * size + size, size), 2 * size), :]
        own = conv[half, 1, here_rows, :]
        out = jnp.zeros((size, size), f32)
        inner = jnp.zeros((size, size), f32)
        for member in range(8):
            group = half * 8 + member
            chosen = group_of_lane == member
            band = back_circ[group]
            out = jnp.where(
                chosen,
                jnp.dot(
                    jnp.concatenate((band * prev_b, band * here_b), axis=1),
                    mixed,
                    preferred_element_type=f32,
                ),
                out,
            )
            band = circ[group]
            inner = jnp.where(
                chosen,
                jnp.dot(
                    jnp.concatenate((band * ahead_b, band * beyond_b), axis=1),
                    grads,
                    preferred_element_type=f32,
                ),
                inner,
            )
            outer = nt_dot(jnp.where(chosen, own, jnp.zeros_like(own)), mixed)
            tap_sum[group] += outer[:, :size] * prev + outer[:, size:] * here
        result[half, 0, rows, :] = out.astype(bf16)
        result[half, 1, rows, :] = inner.astype(bf16)

    def conv_back(half, tb):
        columns = pl.ds(pl.multiple_of(conv_block(p) * CONV_WIDTH + half * 128, 128), 128)
        mine = back_out.at[:, :, columns]

        def one(i, carried):
            r = tb * 4 + i
            rows = result.at[half, :, pl.ds(pl.multiple_of(r * ROWS, ROWS), ROWS), :]

            @pl.when(r == p)
            def _():
                pltpu.make_async_copy(rows, mine, recv_sem.at[5]).start()

            @pl.when(r != p)
            def _():
                pltpu.make_async_remote_copy(
                    src_ref=rows,
                    dst_ref=mine,
                    send_sem=send_sem.at[5],
                    recv_sem=recv_sem.at[5],
                    device_id=device_of(z, r),
                    device_id_type=MESH,
                ).start()

            return carried

        lax.fori_loop(0, 4, one, 0)

    def conv_half(half):
        turn = lax.div(p, 4)

        def inner_tile(i, carried):
            tb = 1 + lax.rem(i + turn, 6)
            conv_tile(half, tb)
            conv_back(half, tb)
            return carried

        def edge_tile(i, carried):
            tb = 7 * lax.rem(i + turn, 2)
            conv_tile(half, tb)
            conv_back(half, tb)
            return carried

        lax.fori_loop(0, 6, inner_tile, 0)
        hops[4 + half].wait()
        hops[6 + half].wait()
        lax.fori_loop(0, 2, edge_tile, 0)

    def add_pair(qi, kb, probs, for_query, for_key):
        query = tile_rows(qg.at[0], qi)
        grad = tile_rows(qg.at[1], qi)
        grad_probs = nt_dot(tile_rows(kv.at[1], kb), grad)
        grad_scores = (probs * (grad_probs - stats[qi, 1:2, :])).astype(bf16)
        if for_key:
            rows = pl.ds(pl.multiple_of((kb - REACH) * TILE, TILE), TILE)
            dv_sum[rows, :] += jnp.dot(probs.astype(bf16), grad, preferred_element_type=f32)
            dk_sum[rows, :] += jnp.dot(grad_scores, query, preferred_element_type=f32)
        if for_query:
            dq_sum[...] += lax.dot_general(
                tile_rows(kv.at[0], kb),
                grad_scores,
                (((0,), (0,)), ((), ())),
                preferred_element_type=f32,
            )

    head_lanes = pl.ds(pl.multiple_of(p * HEAD_DIM, HEAD_DIM), HEAD_DIM)

    def query_back(qi):
        mine = grads_out.at[0, :, head_lanes]

        def one(i, carried):
            r = qi * 8 + lax.rem(i + p, 8)
            rows = grads.at[0, pl.ds(pl.multiple_of(r * ROWS, ROWS), ROWS), :]

            @pl.when(r == p)
            def _():
                pltpu.make_async_copy(rows, mine, recv_sem.at[6]).start()

            @pl.when(r != p)
            def _():
                pltpu.make_async_remote_copy(
                    src_ref=rows,
                    dst_ref=mine,
                    send_sem=send_sem.at[6],
                    recv_sem=recv_sem.at[6],
                    device_id=device_of(z, r),
                    device_id_type=MESH,
                ).start()

            return carried

        lax.fori_loop(0, 8, one, 0)

    def own_grads(i, carried):
        qi = lax.rem(i + lax.div(p, 8), NEAR)
        dq_sum[...] = jnp.zeros_like(dq_sum)

        def probs_of(kb):
            slot = qi * REACH + kb
            return saved[slot] * jnp.exp2(tops[slot, 0:1, :] - stats[qi, 0:1, :])

        def before(kb, inner):
            add_pair(qi, kb, probs_of(kb), True, False)
            return inner

        def within(kb, inner):
            add_pair(qi, kb, probs_of(kb), True, True)
            return inner

        lax.fori_loop(qi, REACH, before, 0)
        lax.fori_loop(REACH, REACH + qi + 1, within, 0)
        rows = pl.ds(pl.multiple_of(qi * TILE, TILE), TILE)
        grads[0, rows, :] = (dq_sum[...].T * SCALE).astype(bf16)
        query_back(qi)
        return carried

    def later_grads(qi, carried):
        starts = doc_start(ends, row_positions(z * SPAN + qi * TILE))

        def after(kb, inner):
            s = nt_dot(tile_rows(kv.at[0], kb), tile_rows(qg.at[0], qi)) * LOG2_SCALE
            s = s - stats[qi, 0:1, :]
            probs = jnp.where(seen_before(z, kb, starts), jnp.exp2(s), 0.0)
            add_pair(qi, kb, probs, False, True)
            return inner

        lax.fori_loop(jnp.maximum(qi, REACH), REACH + NEAR, after, 0)
        return carried

    lax.fori_loop(0, NEAR, own_tiles, 0)
    wait_bytes(delta, recv_sem.at[3])
    halo(0)
    conv_half(0)
    halo(1)
    hops[0].wait()
    hops[1].wait()
    lax.fori_loop(0, NEAR, earlier_tiles, 0)
    hop(8, stats.at[pl.ds(0, NEAR)], stats.at[pl.ds(NEAR, NEAR)], 3)
    hop(9, stats.at[pl.ds(0, 1)], stats.at[pl.ds(2 * NEAR, 1)], 2)
    conv_half(1)

    def fold(group, carried):
        total = jnp.zeros((8, size), f32)
        for step in range(size // 8):
            rows = tap_sum[group, 8 * step : 8 * step + 8, :]
            total = total + pltpu.roll(rows, (size - 8 * step) % size, 1)
        folded[group] = total
        return carried

    lax.fori_loop(0, CONV_GROUPS, fold, 0)
    total = folded[:, 0, :]
    for step in range(1, 8):
        total = total + pltpu.roll(folded[:, step, :], size - step, 1)
    taps[0] = total
    dk_sum[...] = jnp.zeros_like(dk_sum)
    dv_sum[...] = jnp.zeros_like(dv_sum)
    for step in range(1, PLANES):
        hop(9 + step, taps.at[0], taps.at[step], step)
    lax.fori_loop(0, NEAR, own_grads, 0)
    for step in range(1, PLANES):
        hops[9 + step].wait()
    tap_total[...] = jnp.dot(
        (taps[0] + taps[1]) + (taps[2] + taps[3]),
        mirror,
        precision=lax.Precision.HIGHEST,
        preferred_element_type=f32,
    )
    hops[8].wait()
    hops[9].wait()
    hops[2].wait()
    hops[3].wait()
    lax.fori_loop(NEAR, NEAR + REACH, later_grads, 0)
    grads[1] = (dk_sum[...] * SCALE).astype(bf16)
    grads[2] = dv_sum[...].astype(bf16)
    send(
        7,
        lambda r: grads.at[pl.ds(1, 2), pl.ds(pl.multiple_of(r * ROWS, ROWS), ROWS), :],
        grads_out.at[pl.ds(1, 2), :, head_lanes],
    )
    tap_rows = taps_out.at[
        pl.ds(pl.multiple_of(lax.div(p, 4) * CONV_GROUPS, CONV_GROUPS), CONV_GROUPS), :
    ]
    pltpu.make_async_copy(tap_total, tap_rows, recv_sem.at[8]).start()

    def tell(i, carried):
        pltpu.make_async_remote_copy(
            src_ref=tap_total,
            dst_ref=tap_rows,
            send_sem=send_sem.at[8],
            recv_sem=recv_sem.at[8],
            device_id=device_of(z, lax.rem(p + 4 * i, PLANE)),
            device_id_type=MESH,
        ).start()
        return carried

    lax.fori_loop(1, PLANE // 4, tell, 0)
    most = PLANE - 1
    wait_bytes(kv.at[:, pl.ds(0, most * ROWS), :], send_sem.at[0])
    wait_bytes(qg.at[:, pl.ds(0, most * ROWS), :], send_sem.at[1])
    wait_bytes(conv.at[0, :, pl.ds(0, most * ROWS), :], send_sem.at[2])
    wait_bytes(delta.at[pl.ds(0, most)], send_sem.at[3])
    wait_bytes(conv.at[1, :, pl.ds(0, most * ROWS), :], send_sem.at[4])
    wait_bytes(back_out.at[:, :, pl.ds(0, most * CONV_WIDTH)], send_sem.at[5])
    wait_bytes(back_out, recv_sem.at[5])
    wait_bytes(grads.at[0, pl.ds(0, most * ROWS), :], send_sem.at[6])
    wait_bytes(grads_out.at[0], recv_sem.at[6])
    wait_bytes(grads.at[pl.ds(1, 2), pl.ds(0, most * ROWS), :], send_sem.at[7])
    wait_bytes(grads_out.at[pl.ds(1, 2)], recv_sem.at[7])
    wait_bytes(taps_out.at[pl.ds(0, FILTER_LEN - CONV_GROUPS), :], send_sem.at[8])
    wait_bytes(taps_out, recv_sem.at[8])


def exchange(doc_lengths, q, k, v, o, g, cq, ck, cv, cg, filt):
    f32, bf16 = jnp.float32, jnp.bfloat16
    any_space = pl.BlockSpec(memory_space=pl.ANY)
    shape = jax.ShapeDtypeStruct
    vmem, dma = pltpu.VMEM, pltpu.SemaphoreType.DMA
    square = (CONV_GROUPS, FILTER_LEN, FILTER_LEN)
    features, channels = PLANE * HEAD_DIM, PLANE * CONV_WIDTH
    return pl.pallas_call(
        exchange_kernel,
        out_shape=(
            shape((3, ROWS, features), bf16),
            shape((2, ROWS, channels), bf16),
            shape((FILTER_LEN, FILTER_LEN), f32),
        ),
        in_specs=[pl.BlockSpec(memory_space=pltpu.SMEM)]
        + [any_space] * 9
        + [pl.BlockSpec(memory_space=pltpu.VMEM)],
        out_specs=(any_space,) * 3,
        scratch_shapes=[
            vmem((2, ROWS, features), bf16),
            vmem((2, ROWS, features), bf16),
            vmem((ROWS, features), bf16),
            vmem((4, ROWS, channels), bf16),
            vmem((2, ROWS, channels), bf16),
            vmem((PLANE, 1, HEAD_DIM), f32),
            vmem((PLANE, 1, HEAD_DIM), f32),
            vmem((2, WINDOW, HEAD_DIM), bf16),
            vmem((2, WINDOW, HEAD_DIM), bf16),
            vmem((2, 2, SPAN + 2 * FILTER_LEN, 128), bf16),
            vmem((2, 2, SPAN, 128), bf16),
            vmem(square, bf16),
            vmem(square, bf16),
            vmem(square, f32),
            vmem((CONV_GROUPS, 8, FILTER_LEN), f32),
            vmem((PLANES, CONV_GROUPS, FILTER_LEN), f32),
            vmem((NEAR + REACH, 8, TILE), f32),
            vmem((NEAR, 8, TILE), f32),
            vmem((NEAR * (REACH + 1), TILE, TILE), f32),
            vmem((NEAR * (REACH + 1), 8, TILE), f32),
            vmem((SPAN, HEAD_DIM), f32),
            vmem((SPAN, HEAD_DIM), f32),
            vmem((HEAD_DIM, TILE), f32),
            vmem((3, SPAN, HEAD_DIM), bf16),
            vmem((CONV_GROUPS, FILTER_LEN), f32),
            dma((9,)), dma((9,)), dma((9,)), dma((13,)), dma((13,)),
        ],
        compiler_params=pltpu.CompilerParams(
            collective_id=0, has_side_effects=True, vmem_limit_bytes=VMEM_LIMIT
        ),
        name="exchange",
    )(doc_lengths, q, k, v, o, g, cq, ck, cv, cg, filt)


def finish_kernel(grads, taps, back, cg, cv, ck, dq, dk, dv, gcq, gck, gcv, taps_out):
    f32, bf16 = jnp.float32, jnp.bfloat16
    dq[...] = grads[0]
    dk[...] = grads[1]
    dv[...] = grads[2]
    taps_out[...] = taps[...]
    gcq[...] = (cg[...].astype(f32) * back[0].astype(f32)).astype(bf16)
    inner = back[1].astype(f32)
    gck[...] = (inner * cv[...].astype(f32)).astype(bf16)
    gcv[...] = (inner * ck[...].astype(f32)).astype(bf16)


FINISH_STEPS = 4


def finish(grads, taps, back, cg, cv, ck):
    features, channels = grads.shape[2], cg.shape[1]

    def rows(width):
        return pl.BlockSpec((ROWS, width // FINISH_STEPS), lambda i: (0, i))

    def stack(count, width):
        return pl.BlockSpec((count, ROWS, width // FINISH_STEPS), lambda i: (0, 0, i))

    taps_spec = pl.BlockSpec((FILTER_LEN // FINISH_STEPS, FILTER_LEN), lambda i: (i, 0))
    attn = jax.ShapeDtypeStruct(grads.shape[1:], grads.dtype)
    conv = jax.ShapeDtypeStruct(cg.shape, cg.dtype)
    return pl.pallas_call(
        finish_kernel,
        grid=(FINISH_STEPS,),
        out_shape=(attn,) * 3 + (conv,) * 3 + (jax.ShapeDtypeStruct(taps.shape, taps.dtype),),
        in_specs=[stack(3, features), taps_spec, stack(2, channels)] + [rows(channels)] * 3,
        out_specs=(rows(features),) * 3 + (rows(channels),) * 3 + (taps_spec,),
        name="finish",
    )(grads, taps, back, cg, cv, ck)


def body(
    attn_query, attn_key, attn_value, attn_output, attn_grad_out,
    conv_query, conv_key, conv_value, conv_grad_out, conv_filter, doc_lengths,
):
    grads, back, taps = exchange(
        doc_lengths, attn_query, attn_key, attn_value, attn_output, attn_grad_out,
        conv_query, conv_key, conv_value, conv_grad_out, conv_filter,
    )
    return finish(grads, taps, back, conv_grad_out, conv_value, conv_key)


def solution(mesh):
    rows = P(("seq", "ch"), None)
    return jax.shard_map(
        body,
        mesh=mesh,
        in_specs=(rows,) * 9 + (P("ch", None), P()),
        out_specs=(rows,) * 6 + (P("ch", None),),
        check_vma=False,
    )
```

```python
import math

import jax
import jax.numpy as jnp
from jax import lax
from jax.experimental import pallas as pl
from jax.experimental.pallas import tpu as pltpu
from jax.sharding import PartitionSpec as P

MESH = pl.DeviceIdType.MESH
HEAD_DIM = 128
FILTER_LEN = 128
DOCS = 12
PLANE = 32
PLANES = 4
ROWS = 32
SPAN = PLANE * ROWS
TILE = 256
NEAR = SPAN // TILE
REACH = 5
WINDOW = SPAN + REACH * TILE
CONV_WIDTH = 256
CONV_GROUPS = 16
LOG2_SCALE = math.log2(math.e) / math.sqrt(HEAD_DIM)
SCALE = 1.0 / math.sqrt(HEAD_DIM)
NEG_FILL = -1e30
VMEM_LIMIT = 60 * 1024 * 1024


def place_in_slice():
    me = lax.axis_index("seq") * 4 + lax.axis_index("ch")
    return lax.div(me, PLANE), lax.rem(me, PLANE)


def device_of(z, p):
    return (z * (PLANE // 4) + lax.div(p, 4), lax.rem(p, 4))


def conv_block(p):
    return lax.rem(p, 4) * (PLANE // 4) + lax.div(p, 4)


def partner(p, i):
    turn, member = lax.div(i, 16), lax.rem(i, 16)
    across = lax.rem(member, 4)
    down = lax.rem(lax.div(member, 4) + 3 * member, 4)
    x = lax.rem(lax.rem(lax.div(p, 2), 4) + across, 4)
    y = lax.rem(lax.div(p, 8) + down, 4)
    return y * 8 + x * 2 + lax.rem(p + turn, 2)


def greet(z, p):
    barrier = pltpu.get_barrier_semaphore()

    def hello(k, carried):
        pl.semaphore_signal(
            barrier, inc=1, device_id=device_of(z, lax.rem(p + k, PLANE)), device_id_type=MESH
        )
        return carried

    lax.fori_loop(1, PLANE, hello, 0)
    for step in range(1, PLANES):
        pl.semaphore_signal(
            barrier, inc=1, device_id=device_of(lax.rem(z + step, PLANES), p), device_id_type=MESH
        )
    pl.semaphore_wait(barrier, PLANE - 1 + PLANES - 1)


def wait_bytes(ref, sem):
    pltpu.make_async_copy(ref, ref, sem).wait()


def doc_ends(len_ref):
    ends = []
    total = jnp.int32(0)
    for d in range(DOCS):
        total = total + len_ref[d]
        ends.append(total)
    return ends


def doc_start(ends, pos):
    start = jnp.zeros_like(pos)
    for end in ends:
        start = jnp.maximum(start, jnp.where(end <= pos, end, 0))
    return start


def doc_stop(ends, pos):
    stop = jnp.full_like(pos, ends[-1])
    for end in ends:
        stop = jnp.minimum(stop, jnp.where(end > pos, end, ends[-1]))
    return stop


def nt_dot(a, b):
    return lax.dot_general(a, b, (((1,), (1,)), ((), ())), preferred_element_type=jnp.float32)


def tile_rows(ref, i):
    return ref[pl.ds(pl.multiple_of(i * TILE, TILE), TILE), :]


def row_positions(base):
    return base + lax.broadcasted_iota(jnp.int32, (1, TILE), 1)


def seen_before(z, kb, starts):
    k_pos = z * SPAN - REACH * TILE + kb * TILE + lax.broadcasted_iota(jnp.int32, (TILE, TILE), 0)
    return k_pos >= starts


def seen_diagonal(z, kb, starts):
    below = lax.broadcasted_iota(jnp.int32, (TILE, TILE), 0) <= lax.broadcasted_iota(
        jnp.int32, (TILE, TILE), 1
    )
    return seen_before(z, kb, starts) & below


def exchange_kernel(
    len_ref, q, k, v, o, g, cq, ck, cv, cg, filt,
    grads_out, back_out, taps_out,
    kv_in, qg_in, o_in, conv_in, pair, delta_in, delta, kv, qg, conv, result, circ, back_circ,
    tap_sum, folded, taps, stats, running, saved, tops, dk_sum, dv_sum, dq_sum, grads, tap_total,
    load_sem, send_sem, recv_sem, zsend_sem, zrecv_sem,
):
    z, p = place_in_slice()
    ends = doc_ends(len_ref)
    f32, bf16 = jnp.float32, jnp.bfloat16
    loads = []
    for i, (src, dst) in enumerate(
        (
            (k, kv_in.at[0]), (v, kv_in.at[1]), (q, qg_in.at[0]), (g, qg_in.at[1]), (o, o_in),
            (ck, conv_in.at[0]), (cv, conv_in.at[1]), (cg, conv_in.at[2]), (cq, conv_in.at[3]),
        )
    ):
        copy = pltpu.make_async_copy(src, dst, load_sem.at[i])
        copy.start()
        loads.append(copy)
    greet(z, p)

    def send(slot, take, give):
        pltpu.make_async_copy(take(p), give, recv_sem.at[slot]).start()

        def step(i, carried):
            r = partner(p, i)
            pltpu.make_async_remote_copy(
                src_ref=take(r),
                dst_ref=give,
                send_sem=send_sem.at[slot],
                recv_sem=recv_sem.at[slot],
                device_id=device_of(z, r),
                device_id_type=MESH,
            ).start()
            return carried

        lax.fori_loop(1, PLANE, step, 0)

    hops = {}

    def hop(slot, src, dst, step):
        copy = pltpu.make_async_remote_copy(
            src_ref=src,
            dst_ref=dst,
            send_sem=zsend_sem.at[slot],
            recv_sem=zrecv_sem.at[slot],
            device_id=device_of(lax.rem(z + step, PLANES), p),
            device_id_type=MESH,
        )
        copy.start()
        hops[slot] = copy

    def head_columns(ref, kind):
        return lambda r: ref.at[kind, :, pl.ds(pl.multiple_of(r * HEAD_DIM, HEAD_DIM), HEAD_DIM)]

    def conv_columns(ref, half):
        return lambda r: ref.at[
            :, :, pl.ds(pl.multiple_of(conv_block(r) * CONV_WIDTH + half * 128, 128), 128)
        ]

    def my_rows(base):
        return pl.ds(pl.multiple_of(base + p * ROWS, ROWS), ROWS)

    back = REACH * TILE
    size = FILTER_LEN
    loads[0].wait()
    send(0, head_columns(kv_in, 0), kv.at[0, my_rows(back), :])
    loads[2].wait()
    send(1, head_columns(qg_in, 0), qg.at[0, my_rows(0), :])
    for i in (5, 6, 7, 8):
        loads[i].wait()

    def products(i, carried):
        lanes = pl.ds(pl.multiple_of(i * 512, 512), 512)
        pair[0, :, lanes] = (
            conv_in[0, :, lanes].astype(f32) * conv_in[1, :, lanes].astype(f32)
        ).astype(bf16)
        pair[1, :, lanes] = (
            conv_in[2, :, lanes].astype(f32) * conv_in[3, :, lanes].astype(f32)
        ).astype(bf16)
        return carried

    lax.fori_loop(0, PLANE * CONV_WIDTH // 512, products, 0)
    for i in (1, 3, 4):
        loads[i].wait()

    def deltas(h, carried):
        lanes = pl.ds(pl.multiple_of(h * HEAD_DIM, HEAD_DIM), HEAD_DIM)
        terms = qg_in[1, :, lanes].astype(f32) * o_in[:, lanes].astype(f32)
        padded = jnp.concatenate((terms, jnp.zeros((HEAD_DIM - ROWS, HEAD_DIM), f32)), axis=0)
        delta_in[h] = jnp.sum(padded.T, axis=0, keepdims=True)
        return carried

    lax.fori_loop(0, PLANE, deltas, 0)
    send(9, head_columns(kv_in, 1), kv.at[1, my_rows(back), :])
    send(10, head_columns(qg_in, 1), qg.at[1, my_rows(0), :])
    send(3, lambda r: delta_in.at[r], delta.at[p])

    down = lax.broadcasted_iota(jnp.int32, (size, size), 0)
    across = lax.broadcasted_iota(jnp.int32, (size, size), 1)
    mirror = jnp.where(lax.rem(across + down, size) == 0, 1.0, 0.0)
    own_taps = filt[
        pl.ds(pl.multiple_of(lax.div(p, 4) * CONV_GROUPS, CONV_GROUPS), CONV_GROUPS), :
    ]
    flipped = jnp.dot(own_taps, mirror.astype(bf16), preferred_element_type=f32)
    own_taps = own_taps.astype(f32)
    for group in range(CONV_GROUPS):
        for src, dst in ((own_taps, circ), (flipped, back_circ)):
            row = jnp.broadcast_to(src[group : group + 1, :], (size, size))
            dst[group] = pltpu.roll(row, 0, 1, stride=1, stride_axis=0).astype(bf16)
    tap_sum[...] = jnp.zeros_like(tap_sum)
    stats[0:NEAR] = jnp.zeros((NEAR, 8, TILE), f32)

    def key_hops(kind, near, far):
        hop(near, kv.at[kind, pl.ds(back, SPAN), :], kv.at[kind, pl.ds(TILE, SPAN), :], 1)
        hop(far, kv.at[kind, pl.ds(SPAN + back - TILE, TILE), :], kv.at[kind, pl.ds(0, TILE), :], 2)

    def query_hops(kind, near, far):
        hop(near, qg.at[kind, pl.ds(0, SPAN), :], qg.at[kind, pl.ds(SPAN, SPAN), :], 3)
        hop(far, qg.at[kind, pl.ds(0, TILE), :], qg.at[kind, pl.ds(2 * SPAN, TILE), :], 2)

    def scores(qi, kb, seen):
        starts = doc_start(ends, row_positions(z * SPAN + qi * TILE))
        s = nt_dot(tile_rows(kv.at[0], kb), tile_rows(qg.at[0], qi)) * LOG2_SCALE
        return jnp.where(seen(z, kb, starts), s, NEG_FILL)

    def keep(qi, kb, s, top):
        slot = qi * REACH + kb
        weights = jnp.exp2(s - top)
        saved[slot] = weights
        tops[slot, 0:1, :] = top
        return jnp.sum(weights, axis=0, keepdims=True)

    def extend(qi, kb, state):
        top, total = state
        s = scores(qi, kb, seen_before)
        new_top = jnp.maximum(top, jnp.max(s, axis=0, keepdims=True))
        total = total * jnp.exp2(top - new_top) + keep(qi, kb, s, new_top)
        return new_top, total

    def own_tiles(qi, carried):
        s = scores(qi, qi + REACH, seen_diagonal)
        top = jnp.max(s, axis=0, keepdims=True)
        total = keep(qi, qi + REACH, s, top)
        top, total = lax.fori_loop(
            REACH, REACH + qi, lambda kb, state: extend(qi, kb, state), (top, total)
        )
        running[qi, 0:1, :] = top
        running[qi, 1:2, :] = total
        return carried

    def earlier_tiles(qi, carried):
        top, total = lax.fori_loop(
            qi,
            REACH,
            lambda kb, state: extend(qi, kb, state),
            (running[qi, 0:1, :], running[qi, 1:2, :]),
        )
        stats[qi, 0:1, :] = top + jnp.log2(total)
        for side in range(2):
            row = jnp.zeros((1, HEAD_DIM), f32)
            for part in range(4):
                row = row + pltpu.roll(delta[qi * 8 + side * 4 + part], part * ROWS, 1)
            stats[qi, 1:2, side * HEAD_DIM : (side + 1) * HEAD_DIM] = row
        return carried

    def conv_rows(half, kind, start, count):
        return conv.at[half, kind, pl.ds(start, count), :]

    def halo(half):
        wait_bytes(conv.at[half, :, pl.ds(size, SPAN), :], recv_sem.at[2 + 2 * half])
        hop(4 + half, conv_rows(half, 0, SPAN, size), conv_rows(half, 0, 0, size), 1)
        hop(6 + half, conv_rows(half, 1, size, size), conv_rows(half, 1, SPAN + size, size), 3)

    group_of_lane = lax.div(across, 16)

    def conv_tile(half, tb):
        base = z * SPAN + tb * size
        positions = base + lax.broadcasted_iota(jnp.int32, (1, size), 1)

        def as_column(row):
            return jnp.broadcast_to(row.astype(f32), (size, size)).T.astype(jnp.int32)

        start = as_column(doc_start(ends, positions))
        stop = as_column(doc_stop(ends, positions))
        prev = jnp.where((across > down) & (base - size + across >= start), 1.0, 0.0)
        here = jnp.where((across <= down) & (base + across >= start), 1.0, 0.0)
        ahead = jnp.where((across >= down) & (base + across < stop), 1.0, 0.0)
        beyond = jnp.where((across < down) & (base + size + across < stop), 1.0, 0.0)
        prev_b, here_b = prev.astype(bf16), here.astype(bf16)
        ahead_b, beyond_b = ahead.astype(bf16), beyond.astype(bf16)
        rows = pl.ds(pl.multiple_of(tb * size, size), size)
        here_rows = pl.ds(pl.multiple_of(tb * size + size, size), size)
        mixed = conv[half, 0, pl.ds(pl.multiple_of(tb * size, size), 2 * size), :]
        grads = conv[half, 1, pl.ds(pl.multiple_of(tb * size + size, size), 2 * size), :]
        own = conv[half, 1, here_rows, :]
        out = jnp.zeros((size, size), f32)
        inner = jnp.zeros((size, size), f32)
        for member in range(8):
            group = half * 8 + member
            chosen = group_of_lane == member
            band = back_circ[group]
            out = jnp.where(
                chosen,
                jnp.dot(
                    jnp.concatenate((band * prev_b, band * here_b), axis=1),
                    mixed,
                    preferred_element_type=f32,
                ),
                out,
            )
            band = circ[group]
            inner = jnp.where(
                chosen,
                jnp.dot(
                    jnp.concatenate((band * ahead_b, band * beyond_b), axis=1),
                    grads,
                    preferred_element_type=f32,
                ),
                inner,
            )
            outer = nt_dot(jnp.where(chosen, own, jnp.zeros_like(own)), mixed)
            tap_sum[group] += outer[:, :size] * prev + outer[:, size:] * here
        result[half, 0, rows, :] = out.astype(bf16)
        result[half, 1, rows, :] = inner.astype(bf16)

    def conv_back(half, tb):
        columns = pl.ds(pl.multiple_of(conv_block(p) * CONV_WIDTH + half * 128, 128), 128)
        mine = back_out.at[:, :, columns]

        def one(i, carried):
            r = tb * 4 + i
            rows = result.at[half, :, pl.ds(pl.multiple_of(r * ROWS, ROWS), ROWS), :]

            @pl.when(r == p)
            def _():
                pltpu.make_async_copy(rows, mine, recv_sem.at[5]).start()

            @pl.when(r != p)
            def _():
                pltpu.make_async_remote_copy(
                    src_ref=rows,
                    dst_ref=mine,
                    send_sem=send_sem.at[5],
                    recv_sem=recv_sem.at[5],
                    device_id=device_of(z, r),
                    device_id_type=MESH,
                ).start()

            return carried

        lax.fori_loop(0, 4, one, 0)

    def conv_half(half):
        turn = lax.div(p, 4)

        def inner_tile(i, carried):
            tb = 1 + lax.rem(i + turn, 6)
            conv_tile(half, tb)
            conv_back(half, tb)
            return carried

        def edge_tile(i, carried):
            tb = 7 * lax.rem(i + turn, 2)
            conv_tile(half, tb)
            conv_back(half, tb)
            return carried

        lax.fori_loop(0, 6, inner_tile, 0)
        hops[4 + half].wait()
        hops[6 + half].wait()
        lax.fori_loop(0, 2, edge_tile, 0)

    def add_pair(qi, kb, probs, for_query, for_key):
        query = tile_rows(qg.at[0], qi)
        grad = tile_rows(qg.at[1], qi)
        grad_probs = nt_dot(tile_rows(kv.at[1], kb), grad)
        grad_scores = (probs * (grad_probs - stats[qi, 1:2, :])).astype(bf16)
        if for_key:
            dv_sum[...] += jnp.dot(probs.astype(bf16), grad, preferred_element_type=f32)
            dk_sum[...] += jnp.dot(grad_scores, query, preferred_element_type=f32)
        if for_query:
            dq_sum[qi] += lax.dot_general(
                tile_rows(kv.at[0], kb),
                grad_scores,
                (((0,), (0,)), ((), ())),
                preferred_element_type=f32,
            )

    head_lanes = pl.ds(pl.multiple_of(p * HEAD_DIM, HEAD_DIM), HEAD_DIM)

    def tile_back(slot, kinds, tile):
        mine = grads_out.at[kinds, :, head_lanes]

        def one(i, carried):
            r = tile * 8 + lax.rem(i + p, 8)
            rows = grads.at[kinds, pl.ds(pl.multiple_of(r * ROWS, ROWS), ROWS), :]

            @pl.when(r == p)
            def _():
                pltpu.make_async_copy(rows, mine, recv_sem.at[slot]).start()

            @pl.when(r != p)
            def _():
                pltpu.make_async_remote_copy(
                    src_ref=rows,
                    dst_ref=mine,
                    send_sem=send_sem.at[slot],
                    recv_sem=recv_sem.at[slot],
                    device_id=device_of(z, r),
                    device_id_type=MESH,
                ).start()

            return carried

        lax.fori_loop(0, 8, one, 0)

    def kept_probs(qi, kb):
        slot = qi * REACH + kb
        return saved[slot] * jnp.exp2(tops[slot, 0:1, :] - stats[qi, 0:1, :])

    def later_probs(qi, kb):
        starts = doc_start(ends, row_positions(z * SPAN + qi * TILE))
        s = nt_dot(tile_rows(kv.at[0], kb), tile_rows(qg.at[0], qi)) * LOG2_SCALE
        s = s - stats[qi, 0:1, :]
        return jnp.where(seen_before(z, kb, starts), jnp.exp2(s), 0.0)

    def key_grads(i, carried):
        tile = lax.rem(i + lax.div(p, 8), NEAR)
        kb = tile + REACH
        dk_sum[...] = jnp.zeros_like(dk_sum)
        dv_sum[...] = jnp.zeros_like(dv_sum)

        def within(qi, inner):
            add_pair(qi, kb, kept_probs(qi, kb), True, True)
            return inner

        def after(qi, inner):
            add_pair(qi, kb, later_probs(qi, kb), False, True)
            return inner

        lax.fori_loop(tile, NEAR, within, 0)
        lax.fori_loop(NEAR, kb + 1, after, 0)
        rows = pl.ds(pl.multiple_of(tile * TILE, TILE), TILE)
        grads[1, rows, :] = (dk_sum[...] * SCALE).astype(bf16)
        grads[2, rows, :] = dv_sum[...].astype(bf16)
        tile_back(7, pl.ds(1, 2), tile)
        return carried

    def query_grads(i, carried):
        tile = lax.rem(i + lax.div(p, 8), NEAR)

        def before(kb, inner):
            add_pair(tile, kb, kept_probs(tile, kb), True, False)
            return inner

        lax.fori_loop(tile, REACH, before, 0)
        rows = pl.ds(pl.multiple_of(tile * TILE, TILE), TILE)
        grads[0, rows, :] = (dq_sum[tile].T * SCALE).astype(bf16)
        tile_back(6, pl.ds(0, 1), tile)
        return carried

    wait_bytes(kv.at[0, pl.ds(back, SPAN), :], recv_sem.at[0])
    key_hops(0, 0, 1)
    wait_bytes(qg.at[0, pl.ds(0, SPAN), :], recv_sem.at[1])
    query_hops(0, 2, 3)
    send(2, conv_columns(pair, 0), conv.at[0, :, my_rows(size), :])
    lax.fori_loop(0, NEAR, own_tiles, 0)
    wait_bytes(kv.at[1, pl.ds(back, SPAN), :], recv_sem.at[9])
    wait_bytes(qg.at[1, pl.ds(0, SPAN), :], recv_sem.at[10])
    query_hops(1, 15, 16)
    send(4, conv_columns(pair, 1), conv.at[1, :, my_rows(size), :])
    wait_bytes(delta, recv_sem.at[3])
    hops[0].wait()
    hops[1].wait()
    key_hops(1, 13, 14)
    lax.fori_loop(0, NEAR, earlier_tiles, 0)
    hop(8, stats.at[pl.ds(0, NEAR)], stats.at[pl.ds(NEAR, NEAR)], 3)
    hop(9, stats.at[pl.ds(0, 1)], stats.at[pl.ds(2 * NEAR, 1)], 2)
    halo(0)
    conv_half(0)
    halo(1)
    conv_half(1)

    def fold(group, carried):
        total = jnp.zeros((8, size), f32)
        for step in range(size // 8):
            rows = tap_sum[group, 8 * step : 8 * step + 8, :]
            total = total + pltpu.roll(rows, (size - 8 * step) % size, 1)
        folded[group] = total
        return carried

    lax.fori_loop(0, CONV_GROUPS, fold, 0)
    total = folded[:, 0, :]
    for step in range(1, 8):
        total = total + pltpu.roll(folded[:, step, :], size - step, 1)
    taps[0] = total
    dq_sum[...] = jnp.zeros_like(dq_sum)
    for step in range(1, PLANES):
        hop(9 + step, taps.at[0], taps.at[step], step)
    for slot in (2, 3, 15, 16, 8, 9):
        hops[slot].wait()
    lax.fori_loop(0, NEAR, key_grads, 0)
    for step in range(1, PLANES):
        hops[9 + step].wait()
    tap_total[...] = jnp.dot(
        (taps[0] + taps[1]) + (taps[2] + taps[3]),
        mirror,
        precision=lax.Precision.HIGHEST,
        preferred_element_type=f32,
    )
    hops[13].wait()
    hops[14].wait()
    lax.fori_loop(0, NEAR, query_grads, 0)
    tap_rows = taps_out.at[
        pl.ds(pl.multiple_of(lax.div(p, 4) * CONV_GROUPS, CONV_GROUPS), CONV_GROUPS), :
    ]
    pltpu.make_async_copy(tap_total, tap_rows, recv_sem.at[8]).start()

    def tell(i, carried):
        pltpu.make_async_remote_copy(
            src_ref=tap_total,
            dst_ref=tap_rows,
            send_sem=send_sem.at[8],
            recv_sem=recv_sem.at[8],
            device_id=device_of(z, lax.rem(p + 4 * i, PLANE)),
            device_id_type=MESH,
        ).start()
        return carried

    lax.fori_loop(1, PLANE // 4, tell, 0)
    most = PLANE - 1
    for slot in (0, 1, 9, 10):
        wait_bytes(kv.at[0, pl.ds(0, most * ROWS), :], send_sem.at[slot])
    wait_bytes(conv.at[0, :, pl.ds(0, most * ROWS), :], send_sem.at[2])
    wait_bytes(delta.at[pl.ds(0, most)], send_sem.at[3])
    wait_bytes(conv.at[1, :, pl.ds(0, most * ROWS), :], send_sem.at[4])
    wait_bytes(back_out.at[:, :, pl.ds(0, most * CONV_WIDTH)], send_sem.at[5])
    wait_bytes(back_out, recv_sem.at[5])
    wait_bytes(grads.at[pl.ds(0, 1), pl.ds(0, most * ROWS), :], send_sem.at[6])
    wait_bytes(grads_out.at[pl.ds(0, 1)], recv_sem.at[6])
    wait_bytes(grads.at[pl.ds(1, 2), pl.ds(0, most * ROWS), :], send_sem.at[7])
    wait_bytes(grads_out.at[pl.ds(1, 2)], recv_sem.at[7])
    wait_bytes(taps_out.at[pl.ds(0, FILTER_LEN - CONV_GROUPS), :], send_sem.at[8])
    wait_bytes(taps_out, recv_sem.at[8])


def exchange(doc_lengths, q, k, v, o, g, cq, ck, cv, cg, filt):
    f32, bf16 = jnp.float32, jnp.bfloat16
    any_space = pl.BlockSpec(memory_space=pl.ANY)
    shape = jax.ShapeDtypeStruct
    vmem, dma = pltpu.VMEM, pltpu.SemaphoreType.DMA
    square = (CONV_GROUPS, FILTER_LEN, FILTER_LEN)
    features, channels = PLANE * HEAD_DIM, PLANE * CONV_WIDTH
    return pl.pallas_call(
        exchange_kernel,
        out_shape=(
            shape((3, ROWS, features), bf16),
            shape((2, ROWS, channels), bf16),
            shape((FILTER_LEN, FILTER_LEN), f32),
        ),
        in_specs=[pl.BlockSpec(memory_space=pltpu.SMEM)]
        + [any_space] * 9
        + [pl.BlockSpec(memory_space=pltpu.VMEM)],
        out_specs=(any_space,) * 3,
        scratch_shapes=[
            vmem((2, ROWS, features), bf16),
            vmem((2, ROWS, features), bf16),
            vmem((ROWS, features), bf16),
            vmem((4, ROWS, channels), bf16),
            vmem((2, ROWS, channels), bf16),
            vmem((PLANE, 1, HEAD_DIM), f32),
            vmem((PLANE, 1, HEAD_DIM), f32),
            vmem((2, WINDOW, HEAD_DIM), bf16),
            vmem((2, WINDOW, HEAD_DIM), bf16),
            vmem((2, 2, SPAN + 2 * FILTER_LEN, 128), bf16),
            vmem((2, 2, SPAN, 128), bf16),
            vmem(square, bf16),
            vmem(square, bf16),
            vmem(square, f32),
            vmem((CONV_GROUPS, 8, FILTER_LEN), f32),
            vmem((PLANES, CONV_GROUPS, FILTER_LEN), f32),
            vmem((NEAR + REACH, 8, TILE), f32),
            vmem((NEAR, 8, TILE), f32),
            vmem((NEAR * (REACH + 1), TILE, TILE), f32),
            vmem((NEAR * (REACH + 1), 8, TILE), f32),
            vmem((TILE, HEAD_DIM), f32),
            vmem((TILE, HEAD_DIM), f32),
            vmem((NEAR, HEAD_DIM, TILE), f32),
            vmem((3, SPAN, HEAD_DIM), bf16),
            vmem((CONV_GROUPS, FILTER_LEN), f32),
            dma((9,)), dma((11,)), dma((11,)), dma((17,)), dma((17,)),
        ],
        compiler_params=pltpu.CompilerParams(
            collective_id=0, has_side_effects=True, vmem_limit_bytes=VMEM_LIMIT
        ),
        name="exchange",
    )(doc_lengths, q, k, v, o, g, cq, ck, cv, cg, filt)


def finish_kernel(grads, taps, back, cg, cv, ck, dq, dk, dv, gcq, gck, gcv, taps_out):
    f32, bf16 = jnp.float32, jnp.bfloat16
    dq[...] = grads[0]
    dk[...] = grads[1]
    dv[...] = grads[2]
    taps_out[...] = taps[...]
    gcq[...] = (cg[...].astype(f32) * back[0].astype(f32)).astype(bf16)
    inner = back[1].astype(f32)
    gck[...] = (inner * cv[...].astype(f32)).astype(bf16)
    gcv[...] = (inner * ck[...].astype(f32)).astype(bf16)


FINISH_STEPS = 4


def finish(grads, taps, back, cg, cv, ck):
    features, channels = grads.shape[2], cg.shape[1]

    def rows(width):
        return pl.BlockSpec((ROWS, width // FINISH_STEPS), lambda i: (0, i))

    def stack(count, width):
        return pl.BlockSpec((count, ROWS, width // FINISH_STEPS), lambda i: (0, 0, i))

    taps_spec = pl.BlockSpec((FILTER_LEN // FINISH_STEPS, FILTER_LEN), lambda i: (i, 0))
    attn = jax.ShapeDtypeStruct(grads.shape[1:], grads.dtype)
    conv = jax.ShapeDtypeStruct(cg.shape, cg.dtype)
    return pl.pallas_call(
        finish_kernel,
        grid=(FINISH_STEPS,),
        out_shape=(attn,) * 3 + (conv,) * 3 + (jax.ShapeDtypeStruct(taps.shape, taps.dtype),),
        in_specs=[stack(3, features), taps_spec, stack(2, channels)] + [rows(channels)] * 3,
        out_specs=(rows(features),) * 3 + (rows(channels),) * 3 + (taps_spec,),
        name="finish",
    )(grads, taps, back, cg, cv, ck)


def body(
    attn_query, attn_key, attn_value, attn_output, attn_grad_out,
    conv_query, conv_key, conv_value, conv_grad_out, conv_filter, doc_lengths,
):
    grads, back, taps = exchange(
        doc_lengths, attn_query, attn_key, attn_value, attn_output, attn_grad_out,
        conv_query, conv_key, conv_value, conv_grad_out, conv_filter,
    )
    return finish(grads, taps, back, conv_grad_out, conv_value, conv_key)


def solution(mesh):
    rows = P(("seq", "ch"), None)
    return jax.shard_map(
        body,
        mesh=mesh,
        in_specs=(rows,) * 9 + (P("ch", None), P()),
        out_specs=(rows,) * 6 + (P("ch", None),),
        check_vma=False,
    )
```

```python
import math

import jax
import jax.numpy as jnp
from jax import lax
from jax.experimental import pallas as pl
from jax.experimental.pallas import tpu as pltpu
from jax.sharding import PartitionSpec as P

MESH = pl.DeviceIdType.MESH
HEAD_DIM = 128
FILTER_LEN = 128
DOCS = 12
PLANE = 32
PLANES = 4
ROWS = 32
SPAN = PLANE * ROWS
TILE = 256
NEAR = SPAN // TILE
REACH = 5
WINDOW = SPAN + REACH * TILE
CONV_WIDTH = 256
CONV_GROUPS = 16
LOG2_SCALE = math.log2(math.e) / math.sqrt(HEAD_DIM)
SCALE = 1.0 / math.sqrt(HEAD_DIM)
NEG_FILL = -1e30
VMEM_LIMIT = 60 * 1024 * 1024


def place_in_slice():
    me = lax.axis_index("seq") * 4 + lax.axis_index("ch")
    return lax.div(me, PLANE), lax.rem(me, PLANE)


def device_of(z, p):
    return (z * (PLANE // 4) + lax.div(p, 4), lax.rem(p, 4))


def conv_block(p):
    return lax.rem(p, 4) * (PLANE // 4) + lax.div(p, 4)


def partner(p, i):
    turn, member = lax.div(i, 16), lax.rem(i, 16)
    across = lax.rem(member, 4)
    down = lax.rem(lax.div(member, 4) + 3 * member, 4)
    x = lax.rem(lax.rem(lax.div(p, 2), 4) + across, 4)
    y = lax.rem(lax.div(p, 8) + down, 4)
    return y * 8 + x * 2 + lax.rem(p + turn, 2)


def greet(z, p):
    barrier = pltpu.get_barrier_semaphore()

    def hello(k, carried):
        pl.semaphore_signal(
            barrier, inc=1, device_id=device_of(z, lax.rem(p + k, PLANE)), device_id_type=MESH
        )
        return carried

    lax.fori_loop(1, PLANE, hello, 0)
    for step in range(1, PLANES):
        pl.semaphore_signal(
            barrier, inc=1, device_id=device_of(lax.rem(z + step, PLANES), p), device_id_type=MESH
        )
    pl.semaphore_wait(barrier, PLANE - 1 + PLANES - 1)


def wait_bytes(ref, sem):
    pltpu.make_async_copy(ref, ref, sem).wait()


def doc_ends(len_ref):
    ends = []
    total = jnp.int32(0)
    for d in range(DOCS):
        total = total + len_ref[d]
        ends.append(total)
    return ends


def doc_start(ends, pos):
    start = jnp.zeros_like(pos)
    for end in ends:
        start = jnp.maximum(start, jnp.where(end <= pos, end, 0))
    return start


def doc_stop(ends, pos):
    stop = jnp.full_like(pos, ends[-1])
    for end in ends:
        stop = jnp.minimum(stop, jnp.where(end > pos, end, ends[-1]))
    return stop


def nt_dot(a, b):
    return lax.dot_general(a, b, (((1,), (1,)), ((), ())), preferred_element_type=jnp.float32)


def tile_rows(ref, i):
    return ref[pl.ds(pl.multiple_of(i * TILE, TILE), TILE), :]


def row_positions(base):
    return base + lax.broadcasted_iota(jnp.int32, (1, TILE), 1)


def seen_before(z, kb, starts):
    k_pos = z * SPAN - REACH * TILE + kb * TILE + lax.broadcasted_iota(jnp.int32, (TILE, TILE), 0)
    return k_pos >= starts


def seen_diagonal(z, kb, starts):
    below = lax.broadcasted_iota(jnp.int32, (TILE, TILE), 0) <= lax.broadcasted_iota(
        jnp.int32, (TILE, TILE), 1
    )
    return seen_before(z, kb, starts) & below


def exchange_kernel(
    len_ref, q, k, v, o, g, cq, ck, cv, cg, filt,
    grads_out, back_out, taps_out,
    kv_in, qg_in, o_in, conv_in, pair, delta_in, delta, kv, qg, conv, result, circ, back_circ,
    tap_sum, folded, taps, stats, running, saved, tops, dk_sum, dv_sum, dq_sum, grads, tap_total,
    load_sem, send_sem, recv_sem, zsend_sem, zrecv_sem,
):
    z, p = place_in_slice()
    ends = doc_ends(len_ref)
    f32, bf16 = jnp.float32, jnp.bfloat16
    loads = []
    for i, (src, dst) in enumerate(
        (
            (k, kv_in.at[0]), (v, kv_in.at[1]), (q, qg_in.at[0]), (g, qg_in.at[1]), (o, o_in),
            (ck, conv_in.at[0]), (cv, conv_in.at[1]), (cg, conv_in.at[2]), (cq, conv_in.at[3]),
        )
    ):
        copy = pltpu.make_async_copy(src, dst, load_sem.at[i])
        copy.start()
        loads.append(copy)
    greet(z, p)

    def send(slot, take, give):
        pltpu.make_async_copy(take(p), give, recv_sem.at[slot]).start()

        def step(i, carried):
            r = partner(p, i)
            pltpu.make_async_remote_copy(
                src_ref=take(r),
                dst_ref=give,
                send_sem=send_sem.at[slot],
                recv_sem=recv_sem.at[slot],
                device_id=device_of(z, r),
                device_id_type=MESH,
            ).start()
            return carried

        lax.fori_loop(1, PLANE, step, 0)

    hops = {}

    def hop(slot, src, dst, step):
        copy = pltpu.make_async_remote_copy(
            src_ref=src,
            dst_ref=dst,
            send_sem=zsend_sem.at[slot],
            recv_sem=zrecv_sem.at[slot],
            device_id=device_of(lax.rem(z + step, PLANES), p),
            device_id_type=MESH,
        )
        copy.start()
        hops[slot] = copy

    def head_columns(ref, kind):
        return lambda r: ref.at[kind, :, pl.ds(pl.multiple_of(r * HEAD_DIM, HEAD_DIM), HEAD_DIM)]

    def conv_columns(ref, half):
        return lambda r: ref.at[
            :, :, pl.ds(pl.multiple_of(conv_block(r) * CONV_WIDTH + half * 128, 128), 128)
        ]

    def my_rows(base):
        return pl.ds(pl.multiple_of(base + p * ROWS, ROWS), ROWS)

    back = REACH * TILE
    size = FILTER_LEN
    loads[0].wait()
    send(0, head_columns(kv_in, 0), kv.at[0, my_rows(back), :])
    loads[2].wait()
    send(1, head_columns(qg_in, 0), qg.at[0, my_rows(0), :])
    for i in (5, 6, 7, 8):
        loads[i].wait()

    def products(i, carried):
        lanes = pl.ds(pl.multiple_of(i * 512, 512), 512)
        pair[0, :, lanes] = (
            conv_in[0, :, lanes].astype(f32) * conv_in[1, :, lanes].astype(f32)
        ).astype(bf16)
        pair[1, :, lanes] = (
            conv_in[2, :, lanes].astype(f32) * conv_in[3, :, lanes].astype(f32)
        ).astype(bf16)
        return carried

    lax.fori_loop(0, PLANE * CONV_WIDTH // 512, products, 0)
    for i in (1, 3, 4):
        loads[i].wait()

    def deltas(h, carried):
        lanes = pl.ds(pl.multiple_of(h * HEAD_DIM, HEAD_DIM), HEAD_DIM)
        terms = qg_in[1, :, lanes].astype(f32) * o_in[:, lanes].astype(f32)
        padded = jnp.concatenate((terms, jnp.zeros((HEAD_DIM - ROWS, HEAD_DIM), f32)), axis=0)
        delta_in[h] = jnp.sum(padded.T, axis=0, keepdims=True)
        return carried

    lax.fori_loop(0, PLANE, deltas, 0)
    send(9, head_columns(kv_in, 1), kv.at[1, my_rows(back), :])
    send(10, head_columns(qg_in, 1), qg.at[1, my_rows(0), :])
    send(3, lambda r: delta_in.at[r], delta.at[p])

    down = lax.broadcasted_iota(jnp.int32, (size, size), 0)
    across = lax.broadcasted_iota(jnp.int32, (size, size), 1)
    mirror = jnp.where(lax.rem(across + down, size) == 0, 1.0, 0.0)
    own_taps = filt[
        pl.ds(pl.multiple_of(lax.div(p, 4) * CONV_GROUPS, CONV_GROUPS), CONV_GROUPS), :
    ]
    flipped = jnp.dot(own_taps, mirror.astype(bf16), preferred_element_type=f32)
    own_taps = own_taps.astype(f32)
    for group in range(CONV_GROUPS):
        for src, dst in ((own_taps, circ), (flipped, back_circ)):
            row = jnp.broadcast_to(src[group : group + 1, :], (size, size))
            dst[group] = pltpu.roll(row, 0, 1, stride=1, stride_axis=0).astype(bf16)
    tap_sum[...] = jnp.zeros_like(tap_sum)
    stats[0:NEAR] = jnp.zeros((NEAR, 8, TILE), f32)

    def key_hops(kind, near, far):
        hop(near, kv.at[kind, pl.ds(back, SPAN), :], kv.at[kind, pl.ds(TILE, SPAN), :], 1)
        hop(far, kv.at[kind, pl.ds(SPAN + back - TILE, TILE), :], kv.at[kind, pl.ds(0, TILE), :], 2)

    def query_hops(kind, near, far):
        hop(near, qg.at[kind, pl.ds(0, SPAN), :], qg.at[kind, pl.ds(SPAN, SPAN), :], 3)
        hop(far, qg.at[kind, pl.ds(0, TILE), :], qg.at[kind, pl.ds(2 * SPAN, TILE), :], 2)

    def scores(qi, kb, seen):
        starts = doc_start(ends, row_positions(z * SPAN + qi * TILE))
        s = nt_dot(tile_rows(kv.at[0], kb), tile_rows(qg.at[0], qi)) * LOG2_SCALE
        return jnp.where(seen(z, kb, starts), s, NEG_FILL)

    def keep(qi, kb, s, top):
        slot = qi * REACH + kb
        weights = jnp.exp2(s - top)
        saved[slot] = weights
        tops[slot, 0:1, :] = top
        return jnp.sum(weights, axis=0, keepdims=True)

    def extend(qi, kb, state):
        top, total = state
        s = scores(qi, kb, seen_before)
        new_top = jnp.maximum(top, jnp.max(s, axis=0, keepdims=True))
        total = total * jnp.exp2(top - new_top) + keep(qi, kb, s, new_top)
        return new_top, total

    def own_tiles(qi, carried):
        s = scores(qi, qi + REACH, seen_diagonal)
        top = jnp.max(s, axis=0, keepdims=True)
        total = keep(qi, qi + REACH, s, top)
        top, total = lax.fori_loop(
            REACH, REACH + qi, lambda kb, state: extend(qi, kb, state), (top, total)
        )
        running[qi, 0:1, :] = top
        running[qi, 1:2, :] = total
        return carried

    def earlier_tiles(qi, carried):
        top, total = lax.fori_loop(
            qi,
            REACH,
            lambda kb, state: extend(qi, kb, state),
            (running[qi, 0:1, :], running[qi, 1:2, :]),
        )
        stats[qi, 0:1, :] = top + jnp.log2(total)
        for side in range(2):
            row = jnp.zeros((1, HEAD_DIM), f32)
            for part in range(4):
                row = row + pltpu.roll(delta[qi * 8 + side * 4 + part], part * ROWS, 1)
            stats[qi, 1:2, side * HEAD_DIM : (side + 1) * HEAD_DIM] = row
        return carried

    def conv_rows(half, kind, start, count):
        return conv.at[half, kind, pl.ds(start, count), :]

    def halo(half):
        wait_bytes(conv.at[half, :, pl.ds(size, SPAN), :], recv_sem.at[2 + 2 * half])
        hop(4 + half, conv_rows(half, 0, SPAN, size), conv_rows(half, 0, 0, size), 1)
        hop(6 + half, conv_rows(half, 1, size, size), conv_rows(half, 1, SPAN + size, size), 3)

    group_of_lane = lax.div(across, 16)

    def conv_tile(half, tb):
        base = z * SPAN + tb * size
        positions = base + lax.broadcasted_iota(jnp.int32, (1, size), 1)

        def as_column(row):
            return jnp.broadcast_to(row.astype(f32), (size, size)).T.astype(jnp.int32)

        start = as_column(doc_start(ends, positions))
        stop = as_column(doc_stop(ends, positions))
        prev = jnp.where((across > down) & (base - size + across >= start), 1.0, 0.0)
        here = jnp.where((across <= down) & (base + across >= start), 1.0, 0.0)
        ahead = jnp.where((across >= down) & (base + across < stop), 1.0, 0.0)
        beyond = jnp.where((across < down) & (base + size + across < stop), 1.0, 0.0)
        prev_b, here_b = prev.astype(bf16), here.astype(bf16)
        ahead_b, beyond_b = ahead.astype(bf16), beyond.astype(bf16)
        rows = pl.ds(pl.multiple_of(tb * size, size), size)
        here_rows = pl.ds(pl.multiple_of(tb * size + size, size), size)
        mixed = conv[half, 0, pl.ds(pl.multiple_of(tb * size, size), 2 * size), :]
        grads = conv[half, 1, pl.ds(pl.multiple_of(tb * size + size, size), 2 * size), :]
        own = conv[half, 1, here_rows, :]
        out = jnp.zeros((size, size), f32)
        inner = jnp.zeros((size, size), f32)
        for member in range(8):
            group = half * 8 + member
            chosen = group_of_lane == member
            band = back_circ[group]
            out = jnp.where(
                chosen,
                jnp.dot(
                    jnp.concatenate((band * prev_b, band * here_b), axis=1),
                    mixed,
                    preferred_element_type=f32,
                ),
                out,
            )
            band = circ[group]
            inner = jnp.where(
                chosen,
                jnp.dot(
                    jnp.concatenate((band * ahead_b, band * beyond_b), axis=1),
                    grads,
                    preferred_element_type=f32,
                ),
                inner,
            )
            outer = nt_dot(jnp.where(chosen, own, jnp.zeros_like(own)), mixed)
            tap_sum[group] += outer[:, :size] * prev + outer[:, size:] * here
        result[half, 0, rows, :] = out.astype(bf16)
        result[half, 1, rows, :] = inner.astype(bf16)

    def conv_back(half, tb):
        columns = pl.ds(pl.multiple_of(conv_block(p) * CONV_WIDTH + half * 128, 128), 128)
        mine = back_out.at[:, :, columns]

        def one(i, carried):
            r = tb * 4 + i
            rows = result.at[half, :, pl.ds(pl.multiple_of(r * ROWS, ROWS), ROWS), :]

            @pl.when(r == p)
            def _():
                pltpu.make_async_copy(rows, mine, recv_sem.at[5]).start()

            @pl.when(r != p)
            def _():
                pltpu.make_async_remote_copy(
                    src_ref=rows,
                    dst_ref=mine,
                    send_sem=send_sem.at[5],
                    recv_sem=recv_sem.at[5],
                    device_id=device_of(z, r),
                    device_id_type=MESH,
                ).start()

            return carried

        lax.fori_loop(0, 4, one, 0)

    def conv_half(half):
        turn = lax.div(p, 4)

        def inner_tile(i, carried):
            tb = 1 + lax.rem(i + turn, 6)
            conv_tile(half, tb)
            conv_back(half, tb)
            return carried

        def edge_tile(i, carried):
            tb = 7 * lax.rem(i + turn, 2)
            conv_tile(half, tb)
            conv_back(half, tb)
            return carried

        lax.fori_loop(0, 6, inner_tile, 0)
        hops[4 + half].wait()
        hops[6 + half].wait()
        lax.fori_loop(0, 2, edge_tile, 0)

    def add_pair(qi, kb, probs, for_query, for_key):
        query = tile_rows(qg.at[0], qi)
        grad = tile_rows(qg.at[1], qi)
        grad_probs = nt_dot(tile_rows(kv.at[1], kb), grad)
        grad_scores = (probs * (grad_probs - stats[qi, 1:2, :])).astype(bf16)
        if for_key:
            dv_sum[...] += jnp.dot(probs.astype(bf16), grad, preferred_element_type=f32)
            dk_sum[...] += jnp.dot(grad_scores, query, preferred_element_type=f32)
        if for_query:
            dq_sum[qi] += lax.dot_general(
                tile_rows(kv.at[0], kb),
                grad_scores,
                (((0,), (0,)), ((), ())),
                preferred_element_type=f32,
            )

    head_lanes = pl.ds(pl.multiple_of(p * HEAD_DIM, HEAD_DIM), HEAD_DIM)

    def tile_back(slot, kinds, tile):
        mine = grads_out.at[kinds, :, head_lanes]

        def one(i, carried):
            r = tile * 8 + lax.rem(i + p, 8)
            rows = grads.at[kinds, pl.ds(pl.multiple_of(r * ROWS, ROWS), ROWS), :]

            @pl.when(r == p)
            def _():
                pltpu.make_async_copy(rows, mine, recv_sem.at[slot]).start()

            @pl.when(r != p)
            def _():
                pltpu.make_async_remote_copy(
                    src_ref=rows,
                    dst_ref=mine,
                    send_sem=send_sem.at[slot],
                    recv_sem=recv_sem.at[slot],
                    device_id=device_of(z, r),
                    device_id_type=MESH,
                ).start()

            return carried

        lax.fori_loop(0, 8, one, 0)

    def kept_probs(qi, kb):
        slot = qi * REACH + kb
        return saved[slot] * jnp.exp2(tops[slot, 0:1, :] - stats[qi, 0:1, :])

    def later_probs(qi, kb):
        starts = doc_start(ends, row_positions(z * SPAN + qi * TILE))
        s = nt_dot(tile_rows(kv.at[0], kb), tile_rows(qg.at[0], qi)) * LOG2_SCALE
        s = s - stats[qi, 0:1, :]
        return jnp.where(seen_before(z, kb, starts), jnp.exp2(s), 0.0)

    def key_grads(i, carried):
        tile = lax.rem(i + lax.div(p, 8), NEAR)
        kb = tile + REACH
        dk_sum[...] = jnp.zeros_like(dk_sum)
        dv_sum[...] = jnp.zeros_like(dv_sum)

        def within(qi, inner):
            add_pair(qi, kb, kept_probs(qi, kb), True, True)
            return inner

        def after(qi, inner):
            add_pair(qi, kb, later_probs(qi, kb), False, True)
            return inner

        lax.fori_loop(tile, NEAR, within, 0)
        lax.fori_loop(NEAR, kb + 1, after, 0)
        rows = pl.ds(pl.multiple_of(tile * TILE, TILE), TILE)
        grads[1, rows, :] = (dk_sum[...] * SCALE).astype(bf16)
        grads[2, rows, :] = dv_sum[...].astype(bf16)
        tile_back(7, pl.ds(1, 2), tile)
        return carried

    def query_grads(i, carried):
        tile = lax.rem(i + lax.div(p, 8), NEAR)

        def before(kb, inner):
            add_pair(tile, kb, kept_probs(tile, kb), True, False)
            return inner

        lax.fori_loop(tile, REACH, before, 0)
        rows = pl.ds(pl.multiple_of(tile * TILE, TILE), TILE)
        grads[0, rows, :] = (dq_sum[tile].T * SCALE).astype(bf16)
        tile_back(6, pl.ds(0, 1), tile)
        return carried

    wait_bytes(kv.at[0, pl.ds(back, SPAN), :], recv_sem.at[0])
    key_hops(0, 0, 1)
    wait_bytes(qg.at[0, pl.ds(0, SPAN), :], recv_sem.at[1])
    query_hops(0, 2, 3)
    send(2, conv_columns(pair, 0), conv.at[0, :, my_rows(size), :])
    lax.fori_loop(0, NEAR, own_tiles, 0)
    wait_bytes(kv.at[1, pl.ds(back, SPAN), :], recv_sem.at[9])
    wait_bytes(qg.at[1, pl.ds(0, SPAN), :], recv_sem.at[10])
    query_hops(1, 15, 16)
    send(4, conv_columns(pair, 1), conv.at[1, :, my_rows(size), :])
    wait_bytes(delta, recv_sem.at[3])
    hops[0].wait()
    hops[1].wait()
    key_hops(1, 13, 14)
    lax.fori_loop(0, NEAR, earlier_tiles, 0)
    hop(8, stats.at[pl.ds(0, NEAR)], stats.at[pl.ds(NEAR, NEAR)], 3)
    hop(9, stats.at[pl.ds(0, 1)], stats.at[pl.ds(2 * NEAR, 1)], 2)
    halo(0)
    conv_half(0)
    halo(1)
    conv_half(1)

    def fold(group, carried):
        total = jnp.zeros((8, size), f32)
        for step in range(size // 8):
            rows = tap_sum[group, 8 * step : 8 * step + 8, :]
            total = total + pltpu.roll(rows, (size - 8 * step) % size, 1)
        folded[group] = total
        return carried

    lax.fori_loop(0, CONV_GROUPS, fold, 0)
    total = folded[:, 0, :]
    for step in range(1, 8):
        total = total + pltpu.roll(folded[:, step, :], size - step, 1)
    taps[0] = total
    dq_sum[...] = jnp.zeros_like(dq_sum)
    for step in range(1, PLANES):
        hop(9 + step, taps.at[0], taps.at[step], step)
    for slot in (2, 3, 15, 16, 8, 9):
        hops[slot].wait()
    lax.fori_loop(0, NEAR, key_grads, 0)
    for step in range(1, PLANES):
        hops[9 + step].wait()
    tap_total[...] = jnp.dot(
        (taps[0] + taps[1]) + (taps[2] + taps[3]),
        mirror,
        precision=lax.Precision.HIGHEST,
        preferred_element_type=f32,
    )
    hops[13].wait()
    hops[14].wait()
    lax.fori_loop(0, NEAR, query_grads, 0)
    tap_rows = taps_out.at[
        pl.ds(pl.multiple_of(lax.div(p, 4) * CONV_GROUPS, CONV_GROUPS), CONV_GROUPS), :
    ]
    pltpu.make_async_copy(tap_total, tap_rows, recv_sem.at[8]).start()

    def tell(i, carried):
        pltpu.make_async_remote_copy(
            src_ref=tap_total,
            dst_ref=tap_rows,
            send_sem=send_sem.at[8],
            recv_sem=recv_sem.at[8],
            device_id=device_of(z, lax.rem(p + 4 * i, PLANE)),
            device_id_type=MESH,
        ).start()
        return carried

    lax.fori_loop(1, PLANE // 4, tell, 0)
    most = PLANE - 1
    for slot in (0, 1, 9, 10):
        wait_bytes(kv.at[0, pl.ds(0, most * ROWS), :], send_sem.at[slot])
    wait_bytes(conv.at[0, :, pl.ds(0, most * ROWS), :], send_sem.at[2])
    wait_bytes(delta.at[pl.ds(0, most)], send_sem.at[3])
    wait_bytes(conv.at[1, :, pl.ds(0, most * ROWS), :], send_sem.at[4])
    wait_bytes(back_out.at[:, :, pl.ds(0, most * CONV_WIDTH)], send_sem.at[5])
    wait_bytes(back_out, recv_sem.at[5])
    wait_bytes(grads.at[pl.ds(0, 1), pl.ds(0, most * ROWS), :], send_sem.at[6])
    wait_bytes(grads_out.at[pl.ds(0, 1)], recv_sem.at[6])
    wait_bytes(grads.at[pl.ds(1, 2), pl.ds(0, most * ROWS), :], send_sem.at[7])
    wait_bytes(grads_out.at[pl.ds(1, 2)], recv_sem.at[7])
    wait_bytes(taps_out.at[pl.ds(0, FILTER_LEN - CONV_GROUPS), :], send_sem.at[8])
    wait_bytes(taps_out, recv_sem.at[8])


def exchange(doc_lengths, q, k, v, o, g, cq, ck, cv, cg, filt):
    f32, bf16 = jnp.float32, jnp.bfloat16
    any_space = pl.BlockSpec(memory_space=pl.ANY)
    shape = jax.ShapeDtypeStruct
    vmem, dma = pltpu.VMEM, pltpu.SemaphoreType.DMA
    square = (CONV_GROUPS, FILTER_LEN, FILTER_LEN)
    features, channels = PLANE * HEAD_DIM, PLANE * CONV_WIDTH
    return pl.pallas_call(
        exchange_kernel,
        out_shape=(
            shape((3, ROWS, features), bf16),
            shape((2, ROWS, channels), bf16),
            shape((FILTER_LEN, FILTER_LEN), f32),
        ),
        in_specs=[pl.BlockSpec(memory_space=pltpu.SMEM)]
        + [any_space] * 9
        + [pl.BlockSpec(memory_space=pltpu.VMEM)],
        out_specs=(any_space,) * 3,
        scratch_shapes=[
            vmem((2, ROWS, features), bf16),
            vmem((2, ROWS, features), bf16),
            vmem((ROWS, features), bf16),
            vmem((4, ROWS, channels), bf16),
            vmem((2, ROWS, channels), bf16),
            vmem((PLANE, 1, HEAD_DIM), f32),
            vmem((PLANE, 1, HEAD_DIM), f32),
            vmem((2, WINDOW, HEAD_DIM), bf16),
            vmem((2, WINDOW, HEAD_DIM), bf16),
            vmem((2, 2, SPAN + 2 * FILTER_LEN, 128), bf16),
            vmem((2, 2, SPAN, 128), bf16),
            vmem(square, bf16),
            vmem(square, bf16),
            vmem(square, f32),
            vmem((CONV_GROUPS, 8, FILTER_LEN), f32),
            vmem((PLANES, CONV_GROUPS, FILTER_LEN), f32),
            vmem((NEAR + REACH, 8, TILE), f32),
            vmem((NEAR, 8, TILE), f32),
            vmem((NEAR * (REACH + 1), TILE, TILE), f32),
            vmem((NEAR * (REACH + 1), 8, TILE), f32),
            vmem((TILE, HEAD_DIM), f32),
            vmem((TILE, HEAD_DIM), f32),
            vmem((NEAR, HEAD_DIM, TILE), f32),
            vmem((3, SPAN, HEAD_DIM), bf16),
            vmem((CONV_GROUPS, FILTER_LEN), f32),
            dma((9,)), dma((11,)), dma((11,)), dma((17,)), dma((17,)),
        ],
        compiler_params=pltpu.CompilerParams(
            collective_id=0, has_side_effects=True, vmem_limit_bytes=VMEM_LIMIT
        ),
        name="exchange",
    )(doc_lengths, q, k, v, o, g, cq, ck, cv, cg, filt)


def finish_kernel(grads, taps, back, cg, cv, ck, dq, dk, dv, gcq, gck, gcv, taps_out):
    f32, bf16 = jnp.float32, jnp.bfloat16
    dq[...] = grads[0]
    dk[...] = grads[1]
    dv[...] = grads[2]
    taps_out[...] = taps[...]
    gcq[...] = (cg[...].astype(f32) * back[0].astype(f32)).astype(bf16)
    inner = back[1].astype(f32)
    gck[...] = (inner * cv[...].astype(f32)).astype(bf16)
    gcv[...] = (inner * ck[...].astype(f32)).astype(bf16)


FINISH_STEPS = 2


def finish(grads, taps, back, cg, cv, ck):
    features, channels = grads.shape[2], cg.shape[1]

    def rows(width):
        return pl.BlockSpec((ROWS, width // FINISH_STEPS), lambda i: (0, i))

    def stack(count, width):
        return pl.BlockSpec((count, ROWS, width // FINISH_STEPS), lambda i: (0, 0, i))

    taps_spec = pl.BlockSpec((FILTER_LEN // FINISH_STEPS, FILTER_LEN), lambda i: (i, 0))
    attn = jax.ShapeDtypeStruct(grads.shape[1:], grads.dtype)
    conv = jax.ShapeDtypeStruct(cg.shape, cg.dtype)
    return pl.pallas_call(
        finish_kernel,
        grid=(FINISH_STEPS,),
        out_shape=(attn,) * 3 + (conv,) * 3 + (jax.ShapeDtypeStruct(taps.shape, taps.dtype),),
        in_specs=[stack(3, features), taps_spec, stack(2, channels)] + [rows(channels)] * 3,
        out_specs=(rows(features),) * 3 + (rows(channels),) * 3 + (taps_spec,),
        name="finish",
    )(grads, taps, back, cg, cv, ck)


def body(
    attn_query, attn_key, attn_value, attn_output, attn_grad_out,
    conv_query, conv_key, conv_value, conv_grad_out, conv_filter, doc_lengths,
):
    grads, back, taps = exchange(
        doc_lengths, attn_query, attn_key, attn_value, attn_output, attn_grad_out,
        conv_query, conv_key, conv_value, conv_grad_out, conv_filter,
    )
    return finish(grads, taps, back, conv_grad_out, conv_value, conv_key)


def solution(mesh):
    rows = P(("seq", "ch"), None)
    return jax.shard_map(
        body,
        mesh=mesh,
        in_specs=(rows,) * 9 + (P("ch", None), P()),
        out_specs=(rows,) * 6 + (P("ch", None),),
        check_vma=False,
    )
```

```python
import math

import jax
import jax.numpy as jnp
from jax import lax
from jax.experimental import pallas as pl
from jax.experimental.pallas import tpu as pltpu
from jax.sharding import PartitionSpec as P

MESH = pl.DeviceIdType.MESH
HEAD_DIM = 128
FILTER_LEN = 128
DOCS = 12
PLANE = 32
PLANES = 4
ROWS = 32
SPAN = PLANE * ROWS
TILE = 256
NEAR = SPAN // TILE
REACH = 5
WINDOW = SPAN + REACH * TILE
CONV_WIDTH = 256
CONV_GROUPS = 16
LOG2_SCALE = math.log2(math.e) / math.sqrt(HEAD_DIM)
SCALE = 1.0 / math.sqrt(HEAD_DIM)
NEG_FILL = -1e30
VMEM_LIMIT = 60 * 1024 * 1024


def place_in_slice():
    me = lax.axis_index("seq") * 4 + lax.axis_index("ch")
    return lax.div(me, PLANE), lax.rem(me, PLANE)


def device_of(z, p):
    return (z * (PLANE // 4) + lax.div(p, 4), lax.rem(p, 4))


def conv_block(p):
    return lax.rem(p, 4) * (PLANE // 4) + lax.div(p, 4)


def partner(p, i):
    turn, member = lax.div(i, 16), lax.rem(i, 16)
    across = lax.rem(member, 4)
    down = lax.rem(lax.div(member, 4) + 3 * member, 4)
    x = lax.rem(lax.rem(lax.div(p, 2), 4) + across, 4)
    y = lax.rem(lax.div(p, 8) + down, 4)
    return y * 8 + x * 2 + lax.rem(p + turn, 2)


def greet(z, p):
    barrier = pltpu.get_barrier_semaphore()

    def hello(k, carried):
        pl.semaphore_signal(
            barrier, inc=1, device_id=device_of(z, lax.rem(p + k, PLANE)), device_id_type=MESH
        )
        return carried

    lax.fori_loop(1, PLANE, hello, 0)
    for step in range(1, PLANES):
        pl.semaphore_signal(
            barrier, inc=1, device_id=device_of(lax.rem(z + step, PLANES), p), device_id_type=MESH
        )
    pl.semaphore_wait(barrier, PLANE - 1 + PLANES - 1)


def wait_bytes(ref, sem):
    pltpu.make_async_copy(ref, ref, sem).wait()


def doc_ends(len_ref):
    ends = []
    total = jnp.int32(0)
    for d in range(DOCS):
        total = total + len_ref[d]
        ends.append(total)
    return ends


def doc_start(ends, pos):
    start = jnp.zeros_like(pos)
    for end in ends:
        start = jnp.maximum(start, jnp.where(end <= pos, end, 0))
    return start


def doc_stop(ends, pos):
    stop = jnp.full_like(pos, ends[-1])
    for end in ends:
        stop = jnp.minimum(stop, jnp.where(end > pos, end, ends[-1]))
    return stop


def nt_dot(a, b):
    return lax.dot_general(a, b, (((1,), (1,)), ((), ())), preferred_element_type=jnp.float32)


def tile_rows(ref, i):
    return ref[pl.ds(pl.multiple_of(i * TILE, TILE), TILE), :]


def row_positions(base):
    return base + lax.broadcasted_iota(jnp.int32, (1, TILE), 1)


def seen_before(z, kb, starts):
    k_pos = z * SPAN - REACH * TILE + kb * TILE + lax.broadcasted_iota(jnp.int32, (TILE, TILE), 0)
    return k_pos >= starts


def seen_diagonal(z, kb, starts):
    below = lax.broadcasted_iota(jnp.int32, (TILE, TILE), 0) <= lax.broadcasted_iota(
        jnp.int32, (TILE, TILE), 1
    )
    return seen_before(z, kb, starts) & below


def exchange_kernel(
    len_ref, q, k, v, o, g, cq, ck, cv, cg, filt,
    grads_out, back_out, taps_out,
    kv_in, qg_in, o_in, conv_in, pair, delta_in, delta, kv, qg, conv, result, circ, back_circ,
    tap_sum, folded, taps, stats, running, saved, tops, dk_sum, dv_sum, dq_sum, grads, tap_total, masks, seen_taps,
    load_sem, send_sem, recv_sem, zsend_sem, zrecv_sem,
):
    z, p = place_in_slice()
    ends = doc_ends(len_ref)
    f32, bf16 = jnp.float32, jnp.bfloat16
    loads = []
    for i, (src, dst) in enumerate(
        (
            (k, kv_in.at[0]), (v, kv_in.at[1]), (q, qg_in.at[0]), (g, qg_in.at[1]), (o, o_in),
            (ck, conv_in.at[0]), (cv, conv_in.at[1]), (cg, conv_in.at[2]), (cq, conv_in.at[3]),
        )
    ):
        copy = pltpu.make_async_copy(src, dst, load_sem.at[i])
        copy.start()
        loads.append(copy)
    greet(z, p)

    def send(slot, take, give):
        pltpu.make_async_copy(take(p), give, recv_sem.at[slot]).start()

        def step(i, carried):
            r = partner(p, i)
            pltpu.make_async_remote_copy(
                src_ref=take(r),
                dst_ref=give,
                send_sem=send_sem.at[slot],
                recv_sem=recv_sem.at[slot],
                device_id=device_of(z, r),
                device_id_type=MESH,
            ).start()
            return carried

        lax.fori_loop(1, PLANE, step, 0)

    hops = {}

    def hop(slot, src, dst, step):
        copy = pltpu.make_async_remote_copy(
            src_ref=src,
            dst_ref=dst,
            send_sem=zsend_sem.at[slot],
            recv_sem=zrecv_sem.at[slot],
            device_id=device_of(lax.rem(z + step, PLANES), p),
            device_id_type=MESH,
        )
        copy.start()
        hops[slot] = copy

    def head_columns(ref, kind):
        return lambda r: ref.at[kind, :, pl.ds(pl.multiple_of(r * HEAD_DIM, HEAD_DIM), HEAD_DIM)]

    def conv_columns(ref, half):
        return lambda r: ref.at[
            :, :, pl.ds(pl.multiple_of(conv_block(r) * CONV_WIDTH + half * 128, 128), 128)
        ]

    def my_rows(base):
        return pl.ds(pl.multiple_of(base + p * ROWS, ROWS), ROWS)

    back = REACH * TILE
    size = FILTER_LEN
    loads[0].wait()
    send(0, head_columns(kv_in, 0), kv.at[0, my_rows(back), :])
    loads[2].wait()
    send(1, head_columns(qg_in, 0), qg.at[0, my_rows(0), :])
    for i in (5, 6, 7, 8):
        loads[i].wait()

    def products(i, carried):
        lanes = pl.ds(pl.multiple_of(i * 512, 512), 512)
        pair[0, :, lanes] = (
            conv_in[0, :, lanes].astype(f32) * conv_in[1, :, lanes].astype(f32)
        ).astype(bf16)
        pair[1, :, lanes] = (
            conv_in[2, :, lanes].astype(f32) * conv_in[3, :, lanes].astype(f32)
        ).astype(bf16)
        return carried

    lax.fori_loop(0, PLANE * CONV_WIDTH // 512, products, 0)
    for i in (1, 3, 4):
        loads[i].wait()

    def deltas(h, carried):
        lanes = pl.ds(pl.multiple_of(h * HEAD_DIM, HEAD_DIM), HEAD_DIM)
        terms = qg_in[1, :, lanes].astype(f32) * o_in[:, lanes].astype(f32)
        padded = jnp.concatenate((terms, jnp.zeros((HEAD_DIM - ROWS, HEAD_DIM), f32)), axis=0)
        delta_in[h] = jnp.sum(padded.T, axis=0, keepdims=True)
        return carried

    lax.fori_loop(0, PLANE, deltas, 0)
    send(9, head_columns(kv_in, 1), kv.at[1, my_rows(back), :])
    send(10, head_columns(qg_in, 1), qg.at[1, my_rows(0), :])
    send(3, lambda r: delta_in.at[r], delta.at[p])

    down = lax.broadcasted_iota(jnp.int32, (size, size), 0)
    across = lax.broadcasted_iota(jnp.int32, (size, size), 1)
    mirror = jnp.where(lax.rem(across + down, size) == 0, 1.0, 0.0)
    own_taps = filt[
        pl.ds(pl.multiple_of(lax.div(p, 4) * CONV_GROUPS, CONV_GROUPS), CONV_GROUPS), :
    ]
    flipped = jnp.dot(own_taps, mirror.astype(bf16), preferred_element_type=f32)
    own_taps = own_taps.astype(f32)
    for group in range(CONV_GROUPS):
        for src, dst in ((own_taps, circ), (flipped, back_circ)):
            row = jnp.broadcast_to(src[group : group + 1, :], (size, size))
            dst[group] = pltpu.roll(row, 0, 1, stride=1, stride_axis=0).astype(bf16)
    tap_sum[...] = jnp.zeros_like(tap_sum)
    stats[0:NEAR] = jnp.zeros((NEAR, 8, TILE), f32)

    def key_hops(kind, near, far):
        hop(near, kv.at[kind, pl.ds(back, SPAN), :], kv.at[kind, pl.ds(TILE, SPAN), :], 1)
        hop(far, kv.at[kind, pl.ds(SPAN + back - TILE, TILE), :], kv.at[kind, pl.ds(0, TILE), :], 2)

    def query_hops(kind, near, far):
        hop(near, qg.at[kind, pl.ds(0, SPAN), :], qg.at[kind, pl.ds(SPAN, SPAN), :], 3)
        hop(far, qg.at[kind, pl.ds(0, TILE), :], qg.at[kind, pl.ds(2 * SPAN, TILE), :], 2)

    def scores(qi, kb, seen):
        starts = doc_start(ends, row_positions(z * SPAN + qi * TILE))
        s = nt_dot(tile_rows(kv.at[0], kb), tile_rows(qg.at[0], qi)) * LOG2_SCALE
        return jnp.where(seen(z, kb, starts), s, NEG_FILL)

    def keep(qi, kb, s, top):
        slot = qi * REACH + kb
        weights = jnp.exp2(s - top)
        saved[slot] = weights
        tops[slot, 0:1, :] = top
        return jnp.sum(weights, axis=0, keepdims=True)

    def extend(qi, kb, state):
        top, total = state
        s = scores(qi, kb, seen_before)
        new_top = jnp.maximum(top, jnp.max(s, axis=0, keepdims=True))
        total = total * jnp.exp2(top - new_top) + keep(qi, kb, s, new_top)
        return new_top, total

    def own_tiles(qi, carried):
        s = scores(qi, qi + REACH, seen_diagonal)
        top = jnp.max(s, axis=0, keepdims=True)
        total = keep(qi, qi + REACH, s, top)
        top, total = lax.fori_loop(
            REACH, REACH + qi, lambda kb, state: extend(qi, kb, state), (top, total)
        )
        running[qi, 0:1, :] = top
        running[qi, 1:2, :] = total
        return carried

    def earlier_tiles(qi, carried):
        top, total = lax.fori_loop(
            qi,
            REACH,
            lambda kb, state: extend(qi, kb, state),
            (running[qi, 0:1, :], running[qi, 1:2, :]),
        )
        stats[qi, 0:1, :] = top + jnp.log2(total)
        for side in range(2):
            row = jnp.zeros((1, HEAD_DIM), f32)
            for part in range(4):
                row = row + pltpu.roll(delta[qi * 8 + side * 4 + part], part * ROWS, 1)
            stats[qi, 1:2, side * HEAD_DIM : (side + 1) * HEAD_DIM] = row
        return carried

    def conv_rows(half, kind, start, count):
        return conv.at[half, kind, pl.ds(start, count), :]

    def halo(half):
        wait_bytes(conv.at[half, :, pl.ds(size, SPAN), :], recv_sem.at[2 + 2 * half])
        hop(4 + half, conv_rows(half, 0, SPAN, size), conv_rows(half, 0, 0, size), 1)
        hop(6 + half, conv_rows(half, 1, size, size), conv_rows(half, 1, SPAN + size, size), 3)

    group_of_lane = lax.div(across, 16)

    def conv_tile(half, tb):
        if half == 0:
            base = z * SPAN + tb * size
            positions = base + lax.broadcasted_iota(jnp.int32, (1, size), 1)

            def as_column(row):
                return jnp.broadcast_to(row.astype(f32), (size, size)).T.astype(jnp.int32)

            start = as_column(doc_start(ends, positions))
            stop = as_column(doc_stop(ends, positions))
            prev = jnp.where((across > down) & (base - size + across >= start), 1.0, 0.0)
            here = jnp.where((across <= down) & (base + across >= start), 1.0, 0.0)
            ahead = jnp.where((across >= down) & (base + across < stop), 1.0, 0.0)
            beyond = jnp.where((across < down) & (base + size + across < stop), 1.0, 0.0)
            prev_b, here_b = prev.astype(bf16), here.astype(bf16)
            ahead_b, beyond_b = ahead.astype(bf16), beyond.astype(bf16)
            for kind, mask in enumerate((prev_b, here_b, ahead_b, beyond_b)):
                masks[tb, kind] = mask
            seen = prev + here
            seen_taps[tb] = seen
        else:
            prev_b, here_b, ahead_b, beyond_b = (masks[tb, kind] for kind in range(4))
            seen = seen_taps[tb]
        rows = pl.ds(pl.multiple_of(tb * size, size), size)
        here_rows = pl.ds(pl.multiple_of(tb * size + size, size), size)
        mixed = conv[half, 0, pl.ds(pl.multiple_of(tb * size, size), 2 * size), :]
        grads = conv[half, 1, pl.ds(pl.multiple_of(tb * size + size, size), 2 * size), :]
        own = conv[half, 1, here_rows, :]
        out = jnp.zeros((size, size), f32)
        inner = jnp.zeros((size, size), f32)
        for member in range(8):
            group = half * 8 + member
            chosen = group_of_lane == member
            band = back_circ[group]
            out = jnp.where(
                chosen,
                jnp.dot(
                    jnp.concatenate((band * prev_b, band * here_b), axis=1),
                    mixed,
                    preferred_element_type=f32,
                ),
                out,
            )
            band = circ[group]
            inner = jnp.where(
                chosen,
                jnp.dot(
                    jnp.concatenate((band * ahead_b, band * beyond_b), axis=1),
                    grads,
                    preferred_element_type=f32,
                ),
                inner,
            )
            outer = nt_dot(jnp.where(chosen, own, jnp.zeros_like(own)), mixed)
            tap_sum[group] += jnp.where(across > down, outer[:, :size], outer[:, size:]) * seen
        result[half, 0, rows, :] = out.astype(bf16)
        result[half, 1, rows, :] = inner.astype(bf16)

    def conv_back(half, tb):
        columns = pl.ds(pl.multiple_of(conv_block(p) * CONV_WIDTH + half * 128, 128), 128)
        mine = back_out.at[:, :, columns]

        def one(i, carried):
            r = tb * 4 + i
            rows = result.at[half, :, pl.ds(pl.multiple_of(r * ROWS, ROWS), ROWS), :]

            @pl.when(r == p)
            def _():
                pltpu.make_async_copy(rows, mine, recv_sem.at[5]).start()

            @pl.when(r != p)
            def _():
                pltpu.make_async_remote_copy(
                    src_ref=rows,
                    dst_ref=mine,
                    send_sem=send_sem.at[5],
                    recv_sem=recv_sem.at[5],
                    device_id=device_of(z, r),
                    device_id_type=MESH,
                ).start()

            return carried

        lax.fori_loop(0, 4, one, 0)

    def conv_half(half):
        turn = lax.div(p, 4)

        def inner_tile(i, carried):
            tb = 1 + lax.rem(i + turn, 6)
            conv_tile(half, tb)
            conv_back(half, tb)
            return carried

        def edge_tile(i, carried):
            tb = 7 * lax.rem(i + turn, 2)
            conv_tile(half, tb)
            conv_back(half, tb)
            return carried

        lax.fori_loop(0, 6, inner_tile, 0)
        hops[4 + half].wait()
        hops[6 + half].wait()
        lax.fori_loop(0, 2, edge_tile, 0)

    def add_pair(qi, kb, probs, for_query, for_key):
        query = tile_rows(qg.at[0], qi)
        grad = tile_rows(qg.at[1], qi)
        grad_probs = nt_dot(tile_rows(kv.at[1], kb), grad)
        grad_scores = (probs * (grad_probs - stats[qi, 1:2, :])).astype(bf16)
        if for_key:
            dv_sum[...] += jnp.dot(probs.astype(bf16), grad, preferred_element_type=f32)
            dk_sum[...] += jnp.dot(grad_scores, query, preferred_element_type=f32)
        if for_query:
            dq_sum[qi] += lax.dot_general(
                tile_rows(kv.at[0], kb),
                grad_scores,
                (((0,), (0,)), ((), ())),
                preferred_element_type=f32,
            )

    head_lanes = pl.ds(pl.multiple_of(p * HEAD_DIM, HEAD_DIM), HEAD_DIM)

    def tile_back(slot, kinds, tile):
        mine = grads_out.at[kinds, :, head_lanes]

        def one(i, carried):
            r = tile * 8 + lax.rem(i + p, 8)
            rows = grads.at[kinds, pl.ds(pl.multiple_of(r * ROWS, ROWS), ROWS), :]

            @pl.when(r == p)
            def _():
                pltpu.make_async_copy(rows, mine, recv_sem.at[slot]).start()

            @pl.when(r != p)
            def _():
                pltpu.make_async_remote_copy(
                    src_ref=rows,
                    dst_ref=mine,
                    send_sem=send_sem.at[slot],
                    recv_sem=recv_sem.at[slot],
                    device_id=device_of(z, r),
                    device_id_type=MESH,
                ).start()

            return carried

        lax.fori_loop(0, 8, one, 0)

    def kept_probs(qi, kb):
        slot = qi * REACH + kb
        return saved[slot] * jnp.exp2(tops[slot, 0:1, :] - stats[qi, 0:1, :])

    def later_probs(qi, kb):
        starts = doc_start(ends, row_positions(z * SPAN + qi * TILE))
        s = nt_dot(tile_rows(kv.at[0], kb), tile_rows(qg.at[0], qi)) * LOG2_SCALE
        s = s - stats[qi, 0:1, :]
        return jnp.where(seen_before(z, kb, starts), jnp.exp2(s), 0.0)

    def key_grads(i, carried):
        tile = lax.rem(i + lax.div(p, 8), NEAR)
        kb = tile + REACH
        dk_sum[...] = jnp.zeros_like(dk_sum)
        dv_sum[...] = jnp.zeros_like(dv_sum)

        def within(qi, inner):
            add_pair(qi, kb, kept_probs(qi, kb), True, True)
            return inner

        def after(qi, inner):
            add_pair(qi, kb, later_probs(qi, kb), False, True)
            return inner

        lax.fori_loop(tile, NEAR, within, 0)
        lax.fori_loop(NEAR, kb + 1, after, 0)
        rows = pl.ds(pl.multiple_of(tile * TILE, TILE), TILE)
        grads[1, rows, :] = (dk_sum[...] * SCALE).astype(bf16)
        grads[2, rows, :] = dv_sum[...].astype(bf16)
        tile_back(7, pl.ds(1, 2), tile)
        return carried

    def query_grads(i, carried):
        tile = lax.rem(i + lax.div(p, 8), NEAR)

        def before(kb, inner):
            add_pair(tile, kb, kept_probs(tile, kb), True, False)
            return inner

        lax.fori_loop(tile, REACH, before, 0)
        rows = pl.ds(pl.multiple_of(tile * TILE, TILE), TILE)
        grads[0, rows, :] = (dq_sum[tile].T * SCALE).astype(bf16)
        tile_back(6, pl.ds(0, 1), tile)
        return carried

    wait_bytes(kv.at[0, pl.ds(back, SPAN), :], recv_sem.at[0])
    key_hops(0, 0, 1)
    wait_bytes(qg.at[0, pl.ds(0, SPAN), :], recv_sem.at[1])
    query_hops(0, 2, 3)
    send(2, conv_columns(pair, 0), conv.at[0, :, my_rows(size), :])
    lax.fori_loop(0, NEAR, own_tiles, 0)
    wait_bytes(kv.at[1, pl.ds(back, SPAN), :], recv_sem.at[9])
    wait_bytes(qg.at[1, pl.ds(0, SPAN), :], recv_sem.at[10])
    query_hops(1, 15, 16)
    send(4, conv_columns(pair, 1), conv.at[1, :, my_rows(size), :])
    wait_bytes(delta, recv_sem.at[3])
    hops[0].wait()
    hops[1].wait()
    key_hops(1, 13, 14)
    lax.fori_loop(0, NEAR, earlier_tiles, 0)
    hop(8, stats.at[pl.ds(0, NEAR)], stats.at[pl.ds(NEAR, NEAR)], 3)
    hop(9, stats.at[pl.ds(0, 1)], stats.at[pl.ds(2 * NEAR, 1)], 2)
    halo(0)
    conv_half(0)
    halo(1)
    conv_half(1)

    def fold(group, carried):
        total = jnp.zeros((8, size), f32)
        for step in range(size // 8):
            rows = tap_sum[group, 8 * step : 8 * step + 8, :]
            total = total + pltpu.roll(rows, (size - 8 * step) % size, 1)
        folded[group] = total
        return carried

    lax.fori_loop(0, CONV_GROUPS, fold, 0)
    total = folded[:, 0, :]
    for step in range(1, 8):
        total = total + pltpu.roll(folded[:, step, :], size - step, 1)
    taps[0] = total
    dq_sum[...] = jnp.zeros_like(dq_sum)
    for step in range(1, PLANES):
        hop(9 + step, taps.at[0], taps.at[step], step)
    for slot in (2, 3, 15, 16, 8, 9):
        hops[slot].wait()
    lax.fori_loop(0, NEAR, key_grads, 0)
    for step in range(1, PLANES):
        hops[9 + step].wait()
    tap_total[...] = jnp.dot(
        (taps[0] + taps[1]) + (taps[2] + taps[3]),
        mirror,
        precision=lax.Precision.HIGHEST,
        preferred_element_type=f32,
    )
    hops[13].wait()
    hops[14].wait()
    lax.fori_loop(0, NEAR, query_grads, 0)
    tap_rows = taps_out.at[
        pl.ds(pl.multiple_of(lax.div(p, 4) * CONV_GROUPS, CONV_GROUPS), CONV_GROUPS), :
    ]
    pltpu.make_async_copy(tap_total, tap_rows, recv_sem.at[8]).start()

    def tell(i, carried):
        pltpu.make_async_remote_copy(
            src_ref=tap_total,
            dst_ref=tap_rows,
            send_sem=send_sem.at[8],
            recv_sem=recv_sem.at[8],
            device_id=device_of(z, lax.rem(p + 4 * i, PLANE)),
            device_id_type=MESH,
        ).start()
        return carried

    lax.fori_loop(1, PLANE // 4, tell, 0)
    most = PLANE - 1
    for slot in (0, 1, 9, 10):
        wait_bytes(kv.at[0, pl.ds(0, most * ROWS), :], send_sem.at[slot])
    wait_bytes(conv.at[0, :, pl.ds(0, most * ROWS), :], send_sem.at[2])
    wait_bytes(delta.at[pl.ds(0, most)], send_sem.at[3])
    wait_bytes(conv.at[1, :, pl.ds(0, most * ROWS), :], send_sem.at[4])
    wait_bytes(back_out.at[:, :, pl.ds(0, most * CONV_WIDTH)], send_sem.at[5])
    wait_bytes(back_out, recv_sem.at[5])
    wait_bytes(grads.at[pl.ds(0, 1), pl.ds(0, most * ROWS), :], send_sem.at[6])
    wait_bytes(grads_out.at[pl.ds(0, 1)], recv_sem.at[6])
    wait_bytes(grads.at[pl.ds(1, 2), pl.ds(0, most * ROWS), :], send_sem.at[7])
    wait_bytes(grads_out.at[pl.ds(1, 2)], recv_sem.at[7])
    wait_bytes(taps_out.at[pl.ds(0, FILTER_LEN - CONV_GROUPS), :], send_sem.at[8])
    wait_bytes(taps_out, recv_sem.at[8])


def exchange(doc_lengths, q, k, v, o, g, cq, ck, cv, cg, filt):
    f32, bf16 = jnp.float32, jnp.bfloat16
    any_space = pl.BlockSpec(memory_space=pl.ANY)
    shape = jax.ShapeDtypeStruct
    vmem, dma = pltpu.VMEM, pltpu.SemaphoreType.DMA
    square = (CONV_GROUPS, FILTER_LEN, FILTER_LEN)
    features, channels = PLANE * HEAD_DIM, PLANE * CONV_WIDTH
    return pl.pallas_call(
        exchange_kernel,
        out_shape=(
            shape((3, ROWS, features), bf16),
            shape((2, ROWS, channels), bf16),
            shape((FILTER_LEN, FILTER_LEN), f32),
        ),
        in_specs=[pl.BlockSpec(memory_space=pltpu.SMEM)]
        + [any_space] * 9
        + [pl.BlockSpec(memory_space=pltpu.VMEM)],
        out_specs=(any_space,) * 3,
        scratch_shapes=[
            vmem((2, ROWS, features), bf16),
            vmem((2, ROWS, features), bf16),
            vmem((ROWS, features), bf16),
            vmem((4, ROWS, channels), bf16),
            vmem((2, ROWS, channels), bf16),
            vmem((PLANE, 1, HEAD_DIM), f32),
            vmem((PLANE, 1, HEAD_DIM), f32),
            vmem((2, WINDOW, HEAD_DIM), bf16),
            vmem((2, WINDOW, HEAD_DIM), bf16),
            vmem((2, 2, SPAN + 2 * FILTER_LEN, 128), bf16),
            vmem((2, 2, SPAN, 128), bf16),
            vmem(square, bf16),
            vmem(square, bf16),
            vmem(square, f32),
            vmem((CONV_GROUPS, 8, FILTER_LEN), f32),
            vmem((PLANES, CONV_GROUPS, FILTER_LEN), f32),
            vmem((NEAR + REACH, 8, TILE), f32),
            vmem((NEAR, 8, TILE), f32),
            vmem((NEAR * (REACH + 1), TILE, TILE), f32),
            vmem((NEAR * (REACH + 1), 8, TILE), f32),
            vmem((TILE, HEAD_DIM), f32),
            vmem((TILE, HEAD_DIM), f32),
            vmem((NEAR, HEAD_DIM, TILE), f32),
            vmem((3, SPAN, HEAD_DIM), bf16),
            vmem((CONV_GROUPS, FILTER_LEN), f32),
            vmem((SPAN // FILTER_LEN, 4, FILTER_LEN, FILTER_LEN), bf16),
            vmem((SPAN // FILTER_LEN, FILTER_LEN, FILTER_LEN), f32),
            dma((9,)), dma((11,)), dma((11,)), dma((17,)), dma((17,)),
        ],
        compiler_params=pltpu.CompilerParams(
            collective_id=0, has_side_effects=True, vmem_limit_bytes=VMEM_LIMIT
        ),
        name="exchange",
    )(doc_lengths, q, k, v, o, g, cq, ck, cv, cg, filt)


def finish_kernel(grads, taps, back, cg, cv, ck, dq, dk, dv, gcq, gck, gcv, taps_out):
    f32, bf16 = jnp.float32, jnp.bfloat16
    dq[...] = grads[0]
    dk[...] = grads[1]
    dv[...] = grads[2]
    taps_out[...] = taps[...]
    gcq[...] = (cg[...].astype(f32) * back[0].astype(f32)).astype(bf16)
    inner = back[1].astype(f32)
    gck[...] = (inner * cv[...].astype(f32)).astype(bf16)
    gcv[...] = (inner * ck[...].astype(f32)).astype(bf16)


FINISH_STEPS = 2


def finish(grads, taps, back, cg, cv, ck):
    features, channels = grads.shape[2], cg.shape[1]

    def rows(width):
        return pl.BlockSpec((ROWS, width // FINISH_STEPS), lambda i: (0, i))

    def stack(count, width):
        return pl.BlockSpec((count, ROWS, width // FINISH_STEPS), lambda i: (0, 0, i))

    taps_spec = pl.BlockSpec((FILTER_LEN // FINISH_STEPS, FILTER_LEN), lambda i: (i, 0))
    attn = jax.ShapeDtypeStruct(grads.shape[1:], grads.dtype)
    conv = jax.ShapeDtypeStruct(cg.shape, cg.dtype)
    return pl.pallas_call(
        finish_kernel,
        grid=(FINISH_STEPS,),
        out_shape=(attn,) * 3 + (conv,) * 3 + (jax.ShapeDtypeStruct(taps.shape, taps.dtype),),
        in_specs=[stack(3, features), taps_spec, stack(2, channels)] + [rows(channels)] * 3,
        out_specs=(rows(features),) * 3 + (rows(channels),) * 3 + (taps_spec,),
        name="finish",
    )(grads, taps, back, cg, cv, ck)


def body(
    attn_query, attn_key, attn_value, attn_output, attn_grad_out,
    conv_query, conv_key, conv_value, conv_grad_out, conv_filter, doc_lengths,
):
    grads, back, taps = exchange(
        doc_lengths, attn_query, attn_key, attn_value, attn_output, attn_grad_out,
        conv_query, conv_key, conv_value, conv_grad_out, conv_filter,
    )
    return finish(grads, taps, back, conv_grad_out, conv_value, conv_key)


def solution(mesh):
    rows = P(("seq", "ch"), None)
    return jax.shard_map(
        body,
        mesh=mesh,
        in_specs=(rows,) * 9 + (P("ch", None), P()),
        out_specs=(rows,) * 6 + (P("ch", None),),
        check_vma=False,
    )
```
